32 devices in a mesh: node: 8 (over z, y), local: 4 (over x, core).
Axes of the slice: x: 2, y: 2, z: 4, core: 2. Of those that a mesh axis runs over, the one named last changes fastest.
Arguments:
- tokens: bfloat16 [4096, 4096], P(('node', 'local')), may hold values from -6 to 6
- key_codes: bfloat16 [4096, 512], P('local'), may hold values from -0.09375 to 0.09375
- key_exponents: int32 [4096, 2], P('local'), may hold values from -1 to 1
- key_cotangent: bfloat16 [4096, 512], P(('node', 'local')), may hold values from -6 to 6
Outputs:
- keys: bfloat16 [4096, 512], P(('node', 'local'))
- input_grad: bfloat16 [4096, 4096], P(('node', 'local'))
- weight_grad: float32 [4096, 512], P(('node', 'local'))
The draws below stay inside these ranges and needn't reach their ends.
Inputs may be any that keep to these rules, and one draw needn't show every extreme that they name: key_exponents gives the power of two that scales each block of 256 columns of a row of key_codes.
All inputs are finite; a program needn't handle non-finite values.
Results may differ from the reference program's by a relative error of at most 0.015.
Values may be sent and summed in bfloat16 or wider, within the bound.
A program may use at most 128 MiB of HBM per device.

```python
import math
import jax
import jax.numpy as jnp
from jax import lax

DW = 4096
KVH = 4
HEAD = 128
QBLOCK = 256
SEQ = 8192
TOK_DEV = 128
KV = 512
TOKENS = 4096
N_NODE = 8
N_LOCAL = 4


def touch_ends(array, rng, smallest, high):
    longest = array.shape.index(max(array.shape))
    spots = []
    for shift in (0, 1):
        where = [jax.random.randint(jax.random.fold_in(rng, axis), (), 0, length) for axis, length in enumerate(array.shape)]
        where[longest] = (where[longest] + shift) % array.shape[longest]
        spots.append(tuple(where))
    return array.at[spots[0]].set(smallest).at[spots[1]].set(high)


def with_spikes(values, key, source, target, parts, factor):
    owner, partner = [(jnp.arange(values.shape[position]) // (values.shape[position] // parts)).reshape([-1 if axis == position else 1 for axis in range(values.ndim)]) for position in (source, target)]
    chosen = jax.random.permutation(key, parts)[partner]
    strong = (owner == chosen) | (owner == (partner + parts // 2) % parts)
    return jnp.where(strong, factor * values, values)


def block_levels(own_key, dims, split, least, high):
    gain = 1.0
    for axis_at, shards_of in split:
        draws = jax.random.uniform(jax.random.fold_in(jax.random.fold_in(own_key, 6), axis_at), (shards_of,), jnp.float32, least / len(split), high / len(split))
        gain = gain * jnp.repeat(jnp.exp(draws), dims[axis_at] // shards_of).reshape((-1,) + (1,) * (len(dims) - 1 - axis_at))
    return gain


def normal_values(stream_key, extent, spread, reach, cuts=(), kind=jnp.bfloat16):
    entries = spread * jax.random.normal(stream_key, extent, jnp.float32)
    if cuts:
        entries = entries * block_levels(stream_key, extent, cuts, -0.22, 0.18)
    return jnp.clip(entries, -reach, reach).astype(kind)


def bell_draw_with(stream_key, extent, deviation, limit, shards, heavy, held_as=jnp.bfloat16):
    entries = deviation * jax.random.normal(stream_key, extent, jnp.float32)
    if shards:
        entries = entries * block_levels(stream_key, extent, shards, -0.22, 0.18)
    return jnp.clip(with_spikes(entries, jax.random.fold_in(stream_key, 3), *heavy), -limit, limit).astype(held_as)


def setup_inputs(seed: int = 0) -> dict:
    streams_of = jax.random.split(jax.random.key(seed), 5)
    return {
        "tokens": bell_draw_with(streams_of[0], (TOKENS, DW), 1.0, 6.0, ((0, 32),), (0, 1, 32, 2.75)),
        "key_codes": normal_values(streams_of[1], (DW, KV), DW ** -0.5, 0.09375, ((0, 4),)),
        "key_exponents": touch_ends(jax.random.randint(streams_of[2], (DW, KV // QBLOCK), -1, 2), jax.random.fold_in(streams_of[2], 1), -1, 1).astype(jnp.int32),
        "key_cotangent": normal_values(streams_of[3], (TOKENS, KV), 1.0, 6.0, ((0, 32),)),
    }


THETA = 500000.0

def tables(positions):
    inverse = THETA ** (-(jnp.arange(HEAD // 2, dtype=jnp.float32) * 2.0 / HEAD))
    angles = positions.astype(jnp.float32)[:, None] * inverse[None, :]
    return (jnp.cos(angles), jnp.sin(angles))

def rotate(values, cosine, sine_part):
    count = values.shape[0]
    heads = values.reshape(count, KVH, HEAD)
    first_half = heads[:, :, :HEAD // 2]
    second_half = heads[:, :, HEAD // 2:]
    cos_rows = cosine[:, None, :]
    sin_rows = sine_part[:, None, :]
    joined = jnp.concatenate([first_half * cos_rows - second_half * sin_rows, second_half * cos_rows + first_half * sin_rows], axis=2)
    return joined.reshape(count, KVH * HEAD)

def unrotate(values, cosine, sine_part):
    count = values.shape[0]
    heads = values.reshape(count, KVH, HEAD)
    first_half = heads[:, :, :HEAD // 2]
    second_half = heads[:, :, HEAD // 2:]
    cos_rows = cosine[:, None, :]
    sin_rows = sine_part[:, None, :]
    joined = jnp.concatenate([first_half * cos_rows + second_half * sin_rows, second_half * cos_rows - first_half * sin_rows], axis=2)
    return joined.reshape(count, KVH * HEAD)

def quantize(partial_value):
    blocks = partial_value.reshape(partial_value.shape[0], partial_value.shape[1] // QBLOCK, QBLOCK)
    largest = lax.optimization_barrier(jnp.max(jnp.abs(blocks), axis=2))
    block_scale = jnp.exp2(jnp.ceil(jnp.log2(largest + 1e-06)))
    code_values = (blocks / block_scale[:, :, None]).astype(jnp.bfloat16)
    return (code_values, block_scale.astype(jnp.bfloat16))

def dequantize(code_values, block_scale):
    values = code_values.astype(jnp.float32) * block_scale.astype(jnp.float32)[..., None]
    return values.reshape(values.shape[0], values.shape[1] * values.shape[2])

def reference(tokens, key_codes, key_exponents, key_cotangent):
    expanded = jnp.repeat(jnp.exp2(key_exponents.astype(jnp.float32)), QBLOCK, axis=1)
    weights = (key_codes.astype(jnp.float32) * expanded).astype(jnp.bfloat16)
    positions = jnp.arange(TOKENS, dtype=jnp.int32) % SEQ
    cosine, sine_part = tables(positions)
    projected = jnp.dot(tokens, weights, preferred_element_type=jnp.float32)
    keys = rotate(projected, cosine, sine_part).astype(jnp.bfloat16)
    pre_grad = unrotate(key_cotangent.astype(jnp.float32), cosine, sine_part).astype(jnp.bfloat16)
    input_grad = lax.dot_general(pre_grad, weights, (((1,), (1,)), ((), ())), preferred_element_type=jnp.float32).astype(jnp.bfloat16)
    device_count = N_NODE * N_LOCAL

    def accumulate(summed, device_block):
        block_rows, grad_rows = device_block
        partial_value = lax.dot_general(block_rows, grad_rows, (((0,), (0,)), ((), ())), preferred_element_type=jnp.float32)
        code_values, block_scale = quantize(partial_value)
        return (summed + dequantize(code_values, block_scale), None)
    summed, _ = lax.scan(accumulate, jnp.zeros((DW, KV), jnp.float32), (tokens.reshape(device_count, TOK_DEV, DW), pre_grad.reshape(device_count, TOK_DEV, KV)))
    weight_grad = summed * (1.0 / math.sqrt(TOKENS))
    return (keys, input_grad, weight_grad)
```

```python
import functools
import math

import jax
import jax.numpy as jnp
import numpy as np
from jax import lax
from jax.experimental import pallas as pl
from jax.experimental.pallas import tpu as pltpu
from jax.sharding import PartitionSpec as P

KVH = 4
HEAD = 128
QBLOCK = 256
SEQ = 8192
MESH = pl.DeviceIdType.MESH


THETA = 500000.0


def tables(positions):
    inverse = THETA ** (-(jnp.arange(HEAD // 2, dtype=jnp.float32) * 2.0 / HEAD))
    angles = positions.astype(jnp.float32)[:, None] * inverse[None, :]
    return (jnp.cos(angles), jnp.sin(angles))


def rotate(values, cosine, sine_part):
    count = values.shape[0]
    heads = values.reshape(count, KVH, HEAD)
    first_half = heads[:, :, : HEAD // 2]
    second_half = heads[:, :, HEAD // 2 :]
    cos_rows = cosine[:, None, :]
    sin_rows = sine_part[:, None, :]
    joined = jnp.concatenate(
        [
            first_half * cos_rows - second_half * sin_rows,
            second_half * cos_rows + first_half * sin_rows,
        ],
        axis=2,
    )
    return joined.reshape(count, KVH * HEAD)


def unrotate(values, cosine, sine_part):
    count = values.shape[0]
    heads = values.reshape(count, KVH, HEAD)
    first_half = heads[:, :, : HEAD // 2]
    second_half = heads[:, :, HEAD // 2 :]
    cos_rows = cosine[:, None, :]
    sin_rows = sine_part[:, None, :]
    joined = jnp.concatenate(
        [
            first_half * cos_rows + second_half * sin_rows,
            second_half * cos_rows - first_half * sin_rows,
        ],
        axis=2,
    )
    return joined.reshape(count, KVH * HEAD)


def quantize(partial_value):
    blocks = partial_value.reshape(partial_value.shape[0], partial_value.shape[1] // QBLOCK, QBLOCK)
    largest = jnp.max(jnp.abs(blocks), axis=2)
    block_scale = jnp.exp2(jnp.ceil(jnp.log2(largest + 1e-06)))
    code_values = (blocks / block_scale[:, :, None]).astype(jnp.bfloat16)
    return (code_values, block_scale.astype(jnp.bfloat16))


def expand_codes(code_values, block_scale):
    lead = code_values.shape[:-1]
    blocks = code_values.reshape(lead + (block_scale.shape[-1], QBLOCK))
    values = blocks.astype(jnp.float32) * block_scale.astype(jnp.float32)[..., None]
    return values.reshape(lead + (code_values.shape[-1],))


def on_device(tokens, key_codes, key_exponents, key_cotangent):
    node_count = lax.axis_size("node")
    local_count = lax.axis_size("local")
    tok_count = tokens.shape[0]
    width = tokens.shape[1]
    feature_count = key_codes.shape[1]
    expanded = jnp.repeat(jnp.exp2(key_exponents.astype(jnp.float32)), QBLOCK, axis=1)
    shard_weights = (key_codes.astype(jnp.float32) * expanded).astype(jnp.bfloat16)
    weights = lax.all_gather(shard_weights, "local", axis=0, tiled=True)
    device_index = lax.axis_index("node") * local_count + lax.axis_index("local")
    positions = (device_index * tok_count + jnp.arange(tok_count, dtype=jnp.int32)) % SEQ
    cosine, sine_part = tables(positions)
    pre_grad = unrotate(key_cotangent.astype(jnp.float32), cosine, sine_part).astype(jnp.bfloat16)
    partial_value = lax.dot_general(
        tokens, pre_grad, (((0,), (0,)), ((), ())), preferred_element_type=jnp.float32
    )
    code_values, block_scale = quantize(partial_value)
    row_count = width // (node_count * local_count)
    block_count = feature_count // QBLOCK
    code_grid = code_values.reshape(node_count, local_count, row_count, feature_count)
    scale_grid = block_scale.reshape(node_count, local_count, row_count, block_count)
    projected = jnp.dot(tokens, weights, preferred_element_type=jnp.float32)
    keys = rotate(projected, cosine, sine_part).astype(jnp.bfloat16)
    input_grad = lax.dot_general(
        pre_grad, weights, (((1,), (1,)), ((), ())), preferred_element_type=jnp.float32
    ).astype(jnp.bfloat16)
    got_codes, got_scales = (
        lax.all_to_all(code_grid, "local", split_axis=1, concat_axis=1, tiled=True),
        lax.all_to_all(scale_grid, "local", split_axis=1, concat_axis=1, tiled=True),
    )
    node_terms = jnp.sum(expand_codes(got_codes, got_scales), axis=1)
    summed = (
        lax.psum_scatter(node_terms.astype(jnp.bfloat16), "node", scatter_dimension=0, tiled=True)
        .astype(jnp.float32)
        .reshape(row_count, feature_count)
    )
    total_tokens = tok_count * node_count * local_count
    weight_grad = summed * (1.0 / math.sqrt(total_tokens))
    return (keys, input_grad, weight_grad)


def flip(index, distance):
    result = index
    bit = 1
    while bit <= distance:
        if distance & bit:
            result = result + bit - 2 * bit * lax.rem(lax.div(index, bit), 2)
        bit *= 2
    return result


def turn(values, cosine, signed_sine):
    parts = []
    for head in range(values.shape[1] // HEAD):
        piece = values[:, head * HEAD : (head + 1) * HEAD]
        parts.append(piece * cosine + pltpu.roll(piece, HEAD // 2, 1) * signed_sine)
    return jnp.concatenate(parts, axis=1)


CORES = 2
DEPTH = 4
GROUPS = ("S1", "P2z", "P2z")
ROUTES = {
    "S1": {
        (0, 0): ("x", {"z": (1, 0), "y": (0, 1)}),
        (1, 0): ("z", {"y": (1, 1)}),
        (0, 1): ("y", {}),
        (1, 1): ("y", {}),
    },
    "S2": {
        (0, 0): ("x", {"y": (0, 1), "z": (1, 0)}),
        (0, 1): ("y", {"z": (1, 1)}),
        (1, 0): ("z", {}),
        (1, 1): ("z", {}),
    },
    "P2z": {(0, 0): ("x", {"z": (1, 0)}), (1, 0): ("z", {})},
    "P2y": {(0, 0): ("x", {"y": (0, 1)}), (0, 1): ("y", {})},
}
SIZES = {"S1": 4, "S2": 4, "P2z": 2, "P2y": 2}
ORDER = (
    "xw0:00", "ypre", "cpre", "yc3f", "ccols", "cw", "yc2f", "yc3n", "xw1:00", "yc1f", "yc2n", "yc0f", "yc1n",
    "o0", "o1", "o2", "o3",
    "w0:00",
    "rpre",
    "p0", "p1",
    "g3f", "xw2:00",
    "w1:00", "p2",
    "g2f", "p3",
    "g3n", "u0:00", "v0:00",
    "w0:10", "g1f", "g2n",
    "u1:00", "v1:00",
    "s3",
    "g0f", "g1n",
    "w1:10", "w2:00", "u0:10", "v0:10",
    "u1:10", "v1:10", "u2:00", "v2:00",
    "yc0n",
    "w2:10",
    "s2", "s1",
    "u2:10", "v2:10",
    "w0:01", "u0:01", "v0:01",
    "w0:11", "g0n", "u0:11", "v0:11",
    "fin",
)


def fused_kernel(
    tokens_hbm,
    codes_hbm,
    exponents_ref,
    cotangent_ref,
    inverse_ref,
    keys_ref,
    input_grad_ref,
    weight_grad_ref,
    tokens,
    codes,
    columns,
    pre,
    weights,
    out_x,
    in_x,
    out_z,
    in_z,
    kept,
    projected,
    load_sem,
    own_sem,
    column_send,
    column_recv,
    pre_send,
    pre_recv,
    own_send,
    own_recv,
    weight_send,
    weight_recv,
    sum_send,
    sum_recv,
):
    node = lax.axis_index("node")
    local = lax.axis_index("local")
    nodes = lax.axis_size("node")
    locals_ = lax.axis_size("local")
    count = tokens.shape[0]
    row_count = columns.shape[2]
    shard_rows = weights.shape[1]
    unit_rows = shard_rows // sum(SIZES[g] for g in GROUPS)
    total = count * nodes * locals_

    peers = {
        "c": (node, flip(local, 1)),
        "x": (node, flip(local, 2)),
        "y": (flip(node, 1), local),
        "d": (flip(node, 1), flip(local, 1)),
        "z": (flip(node, 2), local),
        "f": (flip(node, 4), local),
    }
    barrier = pltpu.get_barrier_semaphore()
    for peer in peers.values():
        pl.semaphore_signal(barrier, inc=1, device_id=peer, device_id_type=MESH)

    load_codes = pltpu.make_async_copy(codes_hbm, codes, load_sem.at[0])
    load_codes.start()
    load_tokens = pltpu.make_async_copy(tokens_hbm, tokens, load_sem.at[1])
    load_tokens.start()

    def owned(r, far, e=0, d=0):
        first = (flip(node, 2 * r + e) * locals_ + flip(local, 2 * far + d)) * row_count
        return pl.ds(pl.multiple_of(first, row_count), row_count)

    def slot_rows(slot):
        return pl.ds(slot * count, count)

    own = {}
    for r in range(DEPTH):
        for far in range(2):
            k = 2 * r + far
            own[k] = pltpu.make_async_copy(
                tokens_hbm.at[:, owned(r, far)], columns.at[k, slot_rows(0), :], own_sem.at[k]
            )
            own[k].start()

    start = lax.rem((node * locals_ + local) * count, SEQ)
    positions = lax.rem(start + lax.broadcasted_iota(jnp.int32, (count, HEAD), 0), SEQ)
    angles = positions.astype(jnp.float32) * inverse_ref[...]
    cosine = jnp.cos(angles)
    sine = jnp.sin(angles)
    lane = lax.broadcasted_iota(jnp.int32, (count, HEAD), 1)
    signed_sine = jnp.where(lane < HEAD // 2, -sine, sine)
    pre[slot_rows(0), :] = turn(
        cotangent_ref[...].astype(jnp.float32), cosine, -signed_sine
    ).astype(jnp.bfloat16)

    load_codes.wait()
    scale = jnp.left_shift(1, exponents_ref[...] + 15).astype(jnp.float32) * (2.0**-15)
    scale = jnp.transpose(jnp.concatenate([scale] * (8 // scale.shape[0]), axis=0))
    for block in range(codes.shape[1] // QBLOCK):
        lanes = pl.ds(block * QBLOCK, QBLOCK)
        weights[0, :, lanes] = (
            codes[:, lanes].astype(jnp.float32) * scale[:, block : block + 1]
        ).astype(jnp.bfloat16)
    load_tokens.wait()
    projected[...] = jnp.zeros_like(projected)

    sends = []

    def send(src, dst, send_sem, recv_sem, peer):
        copy = pltpu.make_async_remote_copy(
            src_ref=src,
            dst_ref=dst,
            send_sem=send_sem,
            recv_sem=recv_sem,
            device_id=peers[peer],
            device_id_type=MESH,
        )
        copy.start()
        sends.append(copy)
        return copy

    waits = {}

    def send_columns(name, slot, peer, r, far, e, d):
        k = 2 * r + far
        waits[name, k] = send(
            tokens.at[:, owned(r, far, e, d)],
            columns.at[k, slot_rows(slot), :],
            column_send.at[k, slot],
            column_recv.at[k, slot],
            peer,
        )

    def send_pre(source, slot, peer):
        waits["pre", slot] = send(
            pre.at[slot_rows(source), :],
            pre.at[slot_rows(slot), :],
            pre_send.at[slot],
            pre_recv.at[slot],
            peer,
        )

    blocks = 4
    block_rows = shard_rows // blocks

    def use(slot, first, length):
        rows = pl.ds(pl.multiple_of(first, length), length)
        lane_first = flip(local, slot) * shard_rows + first
        lanes = pl.ds(pl.multiple_of(lane_first, length), length)
        block = weights[slot, rows, :]
        input_grad_ref[:, lanes] = lax.dot_general(
            pre[slot_rows(0), :],
            block,
            (((1,), (1,)), ((), ())),
            preferred_element_type=jnp.float32,
        ).astype(jnp.bfloat16)
        projected[...] += jnp.dot(
            tokens[:, lanes], block, preferred_element_type=jnp.float32
        )

    zbit = lax.rem(lax.div(node, 2), 2)
    ybit = lax.rem(node, 2)
    bases = [sum(SIZES[g] for g in GROUPS[:i]) for i in range(len(GROUPS))]

    def unit_first(group, key):
        kind = GROUPS[group]
        dz, dy = key
        zz = 1 - zbit if dz else zbit
        yy = 1 - ybit if dy else ybit
        index = {"S1": 2 * zz + yy, "S2": 2 * zz + yy, "P2z": zz, "P2y": yy}[kind]
        return pl.multiple_of((bases[group] + index) * unit_rows, unit_rows)

    def sem_index(group, key):
        kind = GROUPS[group]
        dz, dy = key
        return bases[group] + {"S1": 2 * dz + dy, "S2": 2 * dz + dy, "P2z": dz, "P2y": dy}[kind]

    def send_unit(source, slot, group, source_key, key, peer):
        rows = pl.ds(unit_first(group, source_key), unit_rows)
        lane_of = {"x": 0, "y": 1, "z": 2, "c": 3}[peer]
        waits["w", slot, group, key] = send(
            weights.at[source, rows, :],
            weights.at[slot, rows, :],
            weight_send.at[lane_of, sem_index(group, source_key)],
            weight_recv.at[slot - 2, sem_index(group, key)],
            peer,
        )

    def piece(r, far):
        k = 2 * r + far
        own[k].wait()
        for name in "cyd":
            waits[name, k].wait_recv()
        return lax.dot_general(
            columns[k], pre[...], (((0,), (0,)), ((), ())), preferred_element_type=jnp.float32
        )

    def run(step):
        head, _, rest = step.partition(":")
        if step == "ypre":
            send_pre(0, 2, "y")
        elif step == "cpre":
            send_pre(0, 1, "c")
        elif step == "rpre":
            waits["pre", 2].wait_recv()
            send_pre(2, 3, "c")
        elif step == "ccols":
            for r in (3, 2, 1, 0):
                for far in (1, 0):
                    send_columns("c", 1, "c", r, far, 0, 1)
        elif step == "cw":
            for b in range(blocks):
                rows = pl.ds(b * block_rows, block_rows)
                waits["own", b] = send(
                    weights.at[0, rows, :],
                    weights.at[1, rows, :],
                    own_send.at[b],
                    own_recv.at[b],
                    "c",
                )
        elif head[:2] == "yc":
            r, far = int(head[2]), head[3] == "f"
            send_columns("y", 2, "y", r, int(far), 1, 0)
            send_columns("d", 3, "d", r, int(far), 1, 1)
        elif head[:2] == "xw":
            group, key = int(head[2:]), (int(rest[0]), int(rest[1]))
            send_unit(0, 2, group, key, key, "x")
        elif head[0] == "o":
            use(0, int(head[1]) * block_rows, block_rows)
        elif head[0] == "p":
            waits["own", int(head[1])].wait_recv()
            use(1, int(head[1]) * block_rows, block_rows)
        elif head[0] == "w":
            group, key = int(head[1:]), (int(rest[0]), int(rest[1]))
            waits["w", 2, group, key].wait_recv()
            for peer, there in ROUTES[GROUPS[group]][key][1].items():
                send_unit(2, 2, group, key, there, peer)
            send_unit(2, 3, group, key, key, "c")
        elif head[0] in "uv":
            group, key = int(head[1:]), (int(rest[0]), int(rest[1]))
            slot = 2 if head[0] == "u" else 3
            if slot == 3:
                waits["w", 3, group, key].wait_recv()
            use(slot, unit_first(group, key), unit_rows)
        elif head[0] == "g":
            r, far = int(head[1]), head[2] == "f"
            if step == "g3f":
                waits["pre", 1].wait_recv()
                waits["pre", 3].wait_recv()
            if far:
                out_x[r] = piece(r, 1).astype(jnp.bfloat16)
                waits["x", r] = send(
                    out_x.at[r], in_x.at[r], sum_send.at[r], sum_recv.at[r], "x"
                )
            else:
                kept[r] = piece(r, 0)
        elif head[0] == "s":
            r = int(head[1])
            waits["x", r].wait_recv()
            value = kept[r] + in_x[r].astype(jnp.float32)
            if r == 2:
                waits["z", 3].wait_recv()
                value = value + in_z[1].astype(jnp.float32)
            slot = {1: 0, 3: 1, 2: 2}[r]
            out_z[slot] = value.astype(jnp.bfloat16)
            waits["z", r] = send(
                out_z.at[slot],
                in_z.at[slot],
                sum_send.at[DEPTH + slot],
                sum_recv.at[DEPTH + slot],
                "f" if r == 2 else "z",
            )
        elif step == "fin":
            keys_ref[...] = turn(projected[...], cosine, signed_sine).astype(jnp.bfloat16)
            waits["x", 0].wait_recv()
            summed = kept[0] + in_x[0].astype(jnp.float32)
            for r, slot in ((1, 0), (2, 2)):
                waits["z", r].wait_recv()
                summed = summed + in_z[slot].astype(jnp.float32)
            weight_grad_ref[...] = summed * (1.0 / math.sqrt(total))
        elif step == "bar":
            pl.semaphore_wait(barrier, len(peers))
        else:
            raise ValueError(step)

    steps = ORDER
    if "bar" not in steps:
        run("bar")
    for step in steps:
        run(step)
    for copy in sends:
        copy.wait_send()


def fused(tokens, key_codes, key_exponents, key_cotangent):
    nodes = lax.axis_size("node")
    locals_ = lax.axis_size("local")
    count, width = tokens.shape
    shard_rows, features = key_codes.shape
    row_count = width // (nodes * locals_)
    units = sum(SIZES[g] for g in GROUPS)
    half = THETA ** (-(np.arange(HEAD // 2) * 2.0 / HEAD))
    inverse = jnp.asarray(np.concatenate([half, half])[None, :], jnp.float32)
    anywhere = pl.BlockSpec(memory_space=pl.ANY)
    vmem = pl.BlockSpec(memory_space=pltpu.VMEM)
    dma = pltpu.SemaphoreType.DMA
    return pl.pallas_call(
        fused_kernel,
        out_shape=(
            pltpu.VMEM((count, features), jnp.bfloat16),
            pltpu.VMEM((count, width), jnp.bfloat16),
            pltpu.VMEM((row_count, features), jnp.float32),
        ),
        in_specs=[anywhere, anywhere, vmem, vmem, vmem],
        out_specs=(vmem, vmem, vmem),
        scratch_shapes=[
            pltpu.VMEM((count, width), jnp.bfloat16),
            pltpu.VMEM((shard_rows, features), jnp.bfloat16),
            pltpu.VMEM((2 * DEPTH, locals_ * count, row_count), jnp.bfloat16),
            pltpu.VMEM((locals_ * count, features), jnp.bfloat16),
            pltpu.VMEM((locals_, shard_rows, features), jnp.bfloat16),
            pltpu.VMEM((DEPTH, row_count, features), jnp.bfloat16),
            pltpu.VMEM((DEPTH, row_count, features), jnp.bfloat16),
            pltpu.VMEM((DEPTH - 1, row_count, features), jnp.bfloat16),
            pltpu.VMEM((DEPTH - 1, row_count, features), jnp.bfloat16),
            pltpu.VMEM((DEPTH, row_count, features), jnp.float32),
            pltpu.VMEM((count, features), jnp.float32),
            dma((2,)),
            dma((2 * DEPTH,)),
            dma((2 * DEPTH, 4)),
            dma((2 * DEPTH, 4)),
            dma((4,)),
            dma((4,)),
            dma((4,)),
            dma((4,)),
            dma((4, units)),
            dma((2, units)),
            dma((2 * DEPTH,)),
            dma((2 * DEPTH,)),
        ],
        compiler_params=pltpu.CompilerParams(collective_id=0, has_side_effects=True),
    )(tokens, key_codes, key_exponents.T, key_cotangent, inverse)


def solution(mesh):
    def body(tokens, key_codes, key_exponents, key_cotangent):
        nodes, locals_ = mesh.shape["node"], mesh.shape["local"]
        row_count = tokens.shape[1] // (nodes * locals_)
        grid = nodes == 2 * DEPTH and locals_ == 2 * CORES
        run = fused if grid and row_count % HEAD == 0 else on_device
        return run(tokens, key_codes, key_exponents, key_cotangent)

    return jax.shard_map(
        body,
        mesh=mesh,
        in_specs=(
            P(("node", "local"), None),
            P("local", None),
            P("local", None),
            P(("node", "local"), None),
        ),
        out_specs=(
            P(("node", "local"), None),
            P(("node", "local"), None),
            P(("node", "local"), None),
        ),
        check_vma=False,
    )
```

```python
import functools
import math

import jax
import jax.numpy as jnp
import numpy as np
from jax import lax
from jax.experimental import pallas as pl
from jax.experimental.pallas import tpu as pltpu
from jax.sharding import PartitionSpec as P

KVH = 4
HEAD = 128
QBLOCK = 256
SEQ = 8192
MESH = pl.DeviceIdType.MESH


THETA = 500000.0


def tables(positions):
    inverse = THETA ** (-(jnp.arange(HEAD // 2, dtype=jnp.float32) * 2.0 / HEAD))
    angles = positions.astype(jnp.float32)[:, None] * inverse[None, :]
    return (jnp.cos(angles), jnp.sin(angles))


def rotate(values, cosine, sine_part):
    count = values.shape[0]
    heads = values.reshape(count, KVH, HEAD)
    first_half = heads[:, :, : HEAD // 2]
    second_half = heads[:, :, HEAD // 2 :]
    cos_rows = cosine[:, None, :]
    sin_rows = sine_part[:, None, :]
    joined = jnp.concatenate(
        [
            first_half * cos_rows - second_half * sin_rows,
            second_half * cos_rows + first_half * sin_rows,
        ],
        axis=2,
    )
    return joined.reshape(count, KVH * HEAD)


def unrotate(values, cosine, sine_part):
    count = values.shape[0]
    heads = values.reshape(count, KVH, HEAD)
    first_half = heads[:, :, : HEAD // 2]
    second_half = heads[:, :, HEAD // 2 :]
    cos_rows = cosine[:, None, :]
    sin_rows = sine_part[:, None, :]
    joined = jnp.concatenate(
        [
            first_half * cos_rows + second_half * sin_rows,
            second_half * cos_rows - first_half * sin_rows,
        ],
        axis=2,
    )
    return joined.reshape(count, KVH * HEAD)


def quantize(partial_value):
    blocks = partial_value.reshape(partial_value.shape[0], partial_value.shape[1] // QBLOCK, QBLOCK)
    largest = jnp.max(jnp.abs(blocks), axis=2)
    block_scale = jnp.exp2(jnp.ceil(jnp.log2(largest + 1e-06)))
    code_values = (blocks / block_scale[:, :, None]).astype(jnp.bfloat16)
    return (code_values, block_scale.astype(jnp.bfloat16))


def expand_codes(code_values, block_scale):
    lead = code_values.shape[:-1]
    blocks = code_values.reshape(lead + (block_scale.shape[-1], QBLOCK))
    values = blocks.astype(jnp.float32) * block_scale.astype(jnp.float32)[..., None]
    return values.reshape(lead + (code_values.shape[-1],))


def on_device(tokens, key_codes, key_exponents, key_cotangent):
    node_count = lax.axis_size("node")
    local_count = lax.axis_size("local")
    tok_count = tokens.shape[0]
    width = tokens.shape[1]
    feature_count = key_codes.shape[1]
    expanded = jnp.repeat(jnp.exp2(key_exponents.astype(jnp.float32)), QBLOCK, axis=1)
    shard_weights = (key_codes.astype(jnp.float32) * expanded).astype(jnp.bfloat16)
    weights = lax.all_gather(shard_weights, "local", axis=0, tiled=True)
    device_index = lax.axis_index("node") * local_count + lax.axis_index("local")
    positions = (device_index * tok_count + jnp.arange(tok_count, dtype=jnp.int32)) % SEQ
    cosine, sine_part = tables(positions)
    pre_grad = unrotate(key_cotangent.astype(jnp.float32), cosine, sine_part).astype(jnp.bfloat16)
    partial_value = lax.dot_general(
        tokens, pre_grad, (((0,), (0,)), ((), ())), preferred_element_type=jnp.float32
    )
    code_values, block_scale = quantize(partial_value)
    row_count = width // (node_count * local_count)
    block_count = feature_count // QBLOCK
    code_grid = code_values.reshape(node_count, local_count, row_count, feature_count)
    scale_grid = block_scale.reshape(node_count, local_count, row_count, block_count)
    projected = jnp.dot(tokens, weights, preferred_element_type=jnp.float32)
    keys = rotate(projected, cosine, sine_part).astype(jnp.bfloat16)
    input_grad = lax.dot_general(
        pre_grad, weights, (((1,), (1,)), ((), ())), preferred_element_type=jnp.float32
    ).astype(jnp.bfloat16)
    got_codes, got_scales = (
        lax.all_to_all(code_grid, "local", split_axis=1, concat_axis=1, tiled=True),
        lax.all_to_all(scale_grid, "local", split_axis=1, concat_axis=1, tiled=True),
    )
    node_terms = jnp.sum(expand_codes(got_codes, got_scales), axis=1)
    summed = (
        lax.psum_scatter(node_terms.astype(jnp.bfloat16), "node", scatter_dimension=0, tiled=True)
        .astype(jnp.float32)
        .reshape(row_count, feature_count)
    )
    total_tokens = tok_count * node_count * local_count
    weight_grad = summed * (1.0 / math.sqrt(total_tokens))
    return (keys, input_grad, weight_grad)


def flip(index, distance):
    result = index
    bit = 1
    while bit <= distance:
        if distance & bit:
            result = result + bit - 2 * bit * lax.rem(lax.div(index, bit), 2)
        bit *= 2
    return result


def turn(values, cosine, signed_sine):
    parts = []
    for head in range(values.shape[1] // HEAD):
        piece = values[:, head * HEAD : (head + 1) * HEAD]
        parts.append(piece * cosine + pltpu.roll(piece, HEAD // 2, 1) * signed_sine)
    return jnp.concatenate(parts, axis=1)


CORES = 2
DEPTH = 4
GROUPS = ('S1', 'P2z', 'P2z')
ROUTES = {
    "S1": {
        (0, 0): ("x", {"z": (1, 0), "y": (0, 1)}),
        (1, 0): ("z", {"y": (1, 1)}),
        (0, 1): ("y", {}),
        (1, 1): ("y", {}),
    },
    "S2": {
        (0, 0): ("x", {"y": (0, 1), "z": (1, 0)}),
        (0, 1): ("y", {"z": (1, 1)}),
        (1, 0): ("z", {}),
        (1, 1): ("z", {}),
    },
    "P2z": {(0, 0): ("x", {"z": (1, 0)}), (1, 0): ("z", {})},
    "P2y": {(0, 0): ("x", {"y": (0, 1)}), (0, 1): ("y", {})},
}
SPLIT = 2
PARTS = 2
SIZES = {"S1": 4, "S2": 4, "P2z": 2, "P2y": 2}
ORDER = (
    "xw1:00", "ypre", "yc2n", "xw2:00", "ccols", "yc3f", "cw", "w1:00.0",
    "yc2f", "p1", "yc3n", "yc1f", "p2", "xw0:00", "yc0f", "rpre",
    "w1:00.1", "cpre", "w2:00.0", "yc1n", "w2:00.1", "g3f", "w0:00.0", "w1:10.1",
    "g2f", "p0", "g2n", "w0:00.1", "w1:10.0", "g3n", "o3", "o1",
    "s00", "g1f", "u0:00", "s01", "w0:10.1", "u1:00", "o2", "w0:10.0",
    "s10", "v0:10", "g1n", "g0f", "s11", "w2:10.0", "s20", "s21",
    "v0:00", "yc0n", "w0:11.1", "w0:01.1", "w0:01.0", "w2:10.1", "u2:10", "u2:00",
    "o0", "u0:01", "w0:11.0", "u0:11", "u1:10", "v2:00", "v0:01", "v1:00",
    "u0:10", "v0:11", "v1:10", "p3", "v2:10", "key", "g0n", "fin",
)


def fused_kernel(
    tokens_hbm,
    codes_hbm,
    exponents_ref,
    cotangent_ref,
    inverse_ref,
    keys_ref,
    input_grad_ref,
    weight_grad_ref,
    tokens,
    codes,
    columns,
    pre,
    weights,
    out_x,
    in_x,
    out_z,
    in_z,
    kept,
    projected,
    load_sem,
    own_sem,
    column_send,
    column_recv,
    pre_send,
    pre_recv,
    own_send,
    own_recv,
    weight_send,
    weight_recv,
    sum_send,
    sum_recv,
    line_send,
    line_recv,
):
    node = lax.axis_index("node")
    local = lax.axis_index("local")
    nodes = lax.axis_size("node")
    locals_ = lax.axis_size("local")
    count = tokens.shape[0]
    row_count = columns.shape[2]
    shard_rows = weights.shape[1]
    features = pre.shape[1]
    unit_rows = shard_rows // sum(SIZES[g] for g in GROUPS)
    part_rows = unit_rows // PARTS
    width = features // SPLIT
    total = count * nodes * locals_

    depth_at = lax.div(node, 2)
    inner = lax.div(depth_at * (DEPTH - 1 - depth_at), 2)
    peers = {
        "c": (node, flip(local, 1)),
        "x": (node, flip(local, 2)),
        "y": (flip(node, 1), local),
        "d": (flip(node, 1), flip(local, 1)),
        "z": (flip(node, 2), local),
    }
    neighbours = len(peers)
    barrier = pltpu.get_barrier_semaphore()
    for peer in peers.values():
        pl.semaphore_signal(barrier, inc=1, device_id=peer, device_id_type=MESH)
    peers["m"] = (flip(node, 6), local)

    @pl.when(inner == 1)
    def _():
        pl.semaphore_signal(barrier, inc=1, device_id=peers["m"], device_id_type=MESH)

    load_codes = pltpu.make_async_copy(codes_hbm, codes, load_sem.at[0])
    load_codes.start()
    load_tokens = pltpu.make_async_copy(tokens_hbm, tokens, load_sem.at[1])
    load_tokens.start()

    def owned(r, far, e=0, d=0):
        first = (flip(node, 2 * r + e) * locals_ + flip(local, 2 * far + d)) * row_count
        return pl.ds(pl.multiple_of(first, row_count), row_count)

    def slot_rows(slot):
        return pl.ds(slot * count, count)

    def lanes_of(k):
        return pl.ds(k * width, width)

    own = {}
    for r in range(DEPTH):
        for far in range(2):
            k = 2 * r + far
            own[k] = pltpu.make_async_copy(
                tokens_hbm.at[:, owned(r, far)], columns.at[k, slot_rows(0), :], own_sem.at[k]
            )
            own[k].start()

    start = lax.rem((node * locals_ + local) * count, SEQ)
    positions = lax.rem(start + lax.broadcasted_iota(jnp.int32, (count, HEAD), 0), SEQ)
    angles = positions.astype(jnp.float32) * inverse_ref[...]
    cosine = jnp.cos(angles)
    sine = jnp.sin(angles)
    lane = lax.broadcasted_iota(jnp.int32, (count, HEAD), 1)
    signed_sine = jnp.where(lane < HEAD // 2, -sine, sine)
    pre[slot_rows(0), :] = turn(
        cotangent_ref[...].astype(jnp.float32), cosine, -signed_sine
    ).astype(jnp.bfloat16)

    load_codes.wait()
    scale = jnp.left_shift(1, exponents_ref[...] + 15).astype(jnp.float32) * (2.0**-15)
    scale = jnp.transpose(jnp.concatenate([scale] * (8 // scale.shape[0]), axis=0))
    for block in range(codes.shape[1] // QBLOCK):
        lanes = pl.ds(block * QBLOCK, QBLOCK)
        weights[0, :, lanes] = (
            codes[:, lanes].astype(jnp.float32) * scale[:, block : block + 1]
        ).astype(jnp.bfloat16)
    load_tokens.wait()
    projected[...] = jnp.zeros_like(projected)

    sends = []
    waits = {}

    def describe(src, dst, send_sem, recv_sem, peer):
        return pltpu.make_async_remote_copy(
            src_ref=src,
            dst_ref=dst,
            send_sem=send_sem,
            recv_sem=recv_sem,
            device_id=peers[peer],
            device_id_type=MESH,
        )

    def send(src, dst, send_sem, recv_sem, peer):
        copy = describe(src, dst, send_sem, recv_sem, peer)
        copy.start()
        sends.append(copy)
        return copy

    def send_columns(name, slot, peer, r, far, e, d):
        k = 2 * r + far
        waits[name, k] = send(
            tokens.at[:, owned(r, far, e, d)],
            columns.at[k, slot_rows(slot), :],
            column_send.at[k, slot],
            column_recv.at[k, slot],
            peer,
        )

    def send_pre(source, slot, peer):
        waits["pre", slot] = send(
            pre.at[slot_rows(source), :],
            pre.at[slot_rows(slot), :],
            pre_send.at[slot],
            pre_recv.at[slot],
            peer,
        )

    blocks = 4
    block_rows = shard_rows // blocks

    def use(slot, first, length):
        rows = pl.ds(pl.multiple_of(first, length), length)
        lane_first = flip(local, slot) * shard_rows + first
        lanes = pl.ds(pl.multiple_of(lane_first, length), length)
        block = weights[slot, rows, :]
        input_grad_ref[:, lanes] = lax.dot_general(
            pre[slot_rows(0), :],
            block,
            (((1,), (1,)), ((), ())),
            preferred_element_type=jnp.float32,
        ).astype(jnp.bfloat16)
        projected[...] += jnp.dot(
            tokens[:, lanes], block, preferred_element_type=jnp.float32
        )

    zbit = lax.rem(depth_at, 2)
    ybit = lax.rem(node, 2)
    bases = [sum(SIZES[g] for g in GROUPS[:i]) for i in range(len(GROUPS))]

    def unit_first(group, key):
        kind = GROUPS[group]
        dz, dy = key
        zz = 1 - zbit if dz else zbit
        yy = 1 - ybit if dy else ybit
        index = {"S1": 2 * zz + yy, "S2": 2 * zz + yy, "P2z": zz, "P2y": yy}[kind]
        return pl.multiple_of((bases[group] + index) * unit_rows, unit_rows)

    def sem_index(group, key):
        kind = GROUPS[group]
        dz, dy = key
        return bases[group] + {"S1": 2 * dz + dy, "S2": 2 * dz + dy, "P2z": dz, "P2y": dy}[kind]

    def send_unit(source, slot, group, source_key, key, part, peer):
        first = unit_first(group, source_key) + part * part_rows
        rows = pl.ds(pl.multiple_of(first, part_rows), part_rows)
        lane_of = {"x": 0, "y": 1, "z": 2, "c": 3}[peer]
        waits["w", slot, group, key, part] = send(
            weights.at[source, rows, :],
            weights.at[slot, rows, :],
            weight_send.at[lane_of, sem_index(group, source_key), part],
            weight_recv.at[slot - 2, sem_index(group, key), part],
            peer,
        )

    def piece(r, far):
        k = 2 * r + far
        own[k].wait()
        for name in "cyd":
            waits[name, k].wait_recv()
        return lax.dot_general(
            columns[k], pre[...], (((0,), (0,)), ((), ())), preferred_element_type=jnp.float32
        )

    line = {}
    for i in range(DEPTH - 1):
        for k in range(SPLIT):
            for middle in range(2):
                slot = i + DEPTH - 1 if middle and i < 2 else i
                line[middle, i, k] = describe(
                    out_z.at[i * SPLIT + k],
                    in_z.at[slot * SPLIT + k],
                    line_send.at[i * SPLIT + k],
                    line_recv.at[slot * SPLIT + k],
                    "m" if middle and i < 2 else "z",
                )
    order_of = ((3, 2, 1), (2, 3, 1))

    def chain(i, k):
        for middle in range(2):

            @pl.when(inner == middle)
            def _():
                r = order_of[middle][i]
                waits["x", r, k].wait_recv()
                value = kept[r, :, lanes_of(k)] + in_x[r * SPLIT + k].astype(jnp.float32)
                if middle:
                    line[0 if i < 2 else 1, i if i < 2 else 0, k].wait_recv()
                    slot = i if i < 2 else DEPTH - 1
                    value = value + in_z[slot * SPLIT + k].astype(jnp.float32)
                out_z[i * SPLIT + k] = value.astype(jnp.bfloat16)
                line[middle, i, k].start()

    gain = 1.0 / math.sqrt(total)

    def finish(k):
        waits["x", 0, k].wait_recv()
        summed = kept[0, :, lanes_of(k)] + in_x[k].astype(jnp.float32)
        line[0, 2, k].wait_recv()
        summed = summed + in_z[2 * SPLIT + k].astype(jnp.float32)
        weight_grad_ref[:, lanes_of(k)] = summed * gain

        @pl.when(inner == 1)
        def _():
            line[1, 1, k].wait_recv()
            last = in_z[DEPTH * SPLIT + k].astype(jnp.float32)
            weight_grad_ref[:, lanes_of(k)] += last * gain

    pre_ready = []

    def run(step):
        head, _, rest = step.partition(":")
        if step == "ypre":
            send_pre(0, 2, "y")
        elif step == "cpre":
            send_pre(0, 1, "c")
        elif step == "rpre":
            waits["pre", 2].wait_recv()
            send_pre(2, 3, "c")
        elif step == "ccols":
            for r in (3, 2, 1, 0):
                for far in (1, 0):
                    send_columns("c", 1, "c", r, far, 0, 1)
        elif step == "cw":
            for b in range(blocks):
                rows = pl.ds(b * block_rows, block_rows)
                waits["own", b] = send(
                    weights.at[0, rows, :],
                    weights.at[1, rows, :],
                    own_send.at[b],
                    own_recv.at[b],
                    "c",
                )
        elif head[:2] == "yc":
            r, far = int(head[2]), int(head[3] == "f")
            send_columns("y", 2, "y", r, far, 1, 0)
            send_columns("d", 3, "d", r, far, 1, 1)
        elif head[:2] == "xw":
            group, key = int(head[2:]), (int(rest[0]), int(rest[1]))
            for part in range(PARTS):
                send_unit(0, 2, group, key, key, part, "x")
        elif head[0] == "o":
            use(0, int(head[1]) * block_rows, block_rows)
        elif head[0] == "p":
            waits["own", int(head[1])].wait_recv()
            use(1, int(head[1]) * block_rows, block_rows)
        elif head[0] == "w":
            group, key = int(head[1:]), (int(rest[0]), int(rest[1]))
            part = int(rest[3])
            waits["w", 2, group, key, part].wait_recv()
            for peer, there in ROUTES[GROUPS[group]][key][1].items():
                send_unit(2, 2, group, key, there, part, peer)
            send_unit(2, 3, group, key, key, part, "c")
        elif head[0] in "uv":
            group, key = int(head[1:]), (int(rest[0]), int(rest[1]))
            slot = 2 if head[0] == "u" else 3
            if slot == 3:
                for part in range(PARTS):
                    waits["w", 3, group, key, part].wait_recv()
            use(slot, unit_first(group, key), unit_rows)
        elif head[0] == "g":
            r, far = int(head[1]), int(head[2] == "f")
            if not pre_ready:
                waits["pre", 1].wait_recv()
                waits["pre", 3].wait_recv()
                pre_ready.append(True)
            value = piece(r, far)
            if far:
                for k in range(SPLIT):
                    at = r * SPLIT + k
                    out_x[at] = value[:, k * width : (k + 1) * width].astype(jnp.bfloat16)
                    waits["x", r, k] = send(
                        out_x.at[at], in_x.at[at], sum_send.at[at], sum_recv.at[at], "x"
                    )
            else:
                kept[r] = value
        elif head[0] == "s":
            chain(int(head[1]), int(head[2]))
        elif step == "key":
            keys_ref[...] = turn(projected[...], cosine, signed_sine).astype(jnp.bfloat16)
        elif step == "fin":
            for k in range(SPLIT):
                finish(k)
        elif step == "bar":
            pl.semaphore_wait(barrier, neighbours + inner)
        else:
            raise ValueError(step)

    steps = ORDER
    if "bar" not in steps:
        run("bar")
    for step in steps:
        run(step)
    for copy in sends:
        copy.wait_send()
    for middle in range(2):

        @pl.when(inner == middle)
        def _():
            for i in range(DEPTH - 1):
                for k in range(SPLIT):
                    line[middle, i, k].wait_send()


def fused(tokens, key_codes, key_exponents, key_cotangent):
    nodes = lax.axis_size("node")
    locals_ = lax.axis_size("local")
    count, width = tokens.shape
    shard_rows, features = key_codes.shape
    row_count = width // (nodes * locals_)
    units = sum(SIZES[g] for g in GROUPS)
    half = THETA ** (-(np.arange(HEAD // 2) * 2.0 / HEAD))
    inverse = jnp.asarray(np.concatenate([half, half])[None, :], jnp.float32)
    anywhere = pl.BlockSpec(memory_space=pl.ANY)
    vmem = pl.BlockSpec(memory_space=pltpu.VMEM)
    dma = pltpu.SemaphoreType.DMA
    return pl.pallas_call(
        fused_kernel,
        out_shape=(
            pltpu.VMEM((count, features), jnp.bfloat16),
            pltpu.VMEM((count, width), jnp.bfloat16),
            pltpu.VMEM((row_count, features), jnp.float32),
        ),
        in_specs=[anywhere, anywhere, vmem, vmem, vmem],
        out_specs=(vmem, vmem, vmem),
        scratch_shapes=[
            pltpu.VMEM((count, width), jnp.bfloat16),
            pltpu.VMEM((shard_rows, features), jnp.bfloat16),
            pltpu.VMEM((2 * DEPTH, locals_ * count, row_count), jnp.bfloat16),
            pltpu.VMEM((locals_ * count, features), jnp.bfloat16),
            pltpu.VMEM((locals_, shard_rows, features), jnp.bfloat16),
            pltpu.VMEM((DEPTH * SPLIT, row_count, features // SPLIT), jnp.bfloat16),
            pltpu.VMEM((DEPTH * SPLIT, row_count, features // SPLIT), jnp.bfloat16),
            pltpu.VMEM((3 * SPLIT, row_count, features // SPLIT), jnp.bfloat16),
            pltpu.VMEM((5 * SPLIT, row_count, features // SPLIT), jnp.bfloat16),
            pltpu.VMEM((DEPTH, row_count, features), jnp.float32),
            pltpu.VMEM((count, features), jnp.float32),
            dma((2,)),
            dma((2 * DEPTH,)),
            dma((2 * DEPTH, 4)),
            dma((2 * DEPTH, 4)),
            dma((4,)),
            dma((4,)),
            dma((4,)),
            dma((4,)),
            dma((4, units, PARTS)),
            dma((2, units, PARTS)),
            dma((DEPTH * SPLIT,)),
            dma((DEPTH * SPLIT,)),
            dma((3 * SPLIT,)),
            dma((5 * SPLIT,)),
        ],
        compiler_params=pltpu.CompilerParams(collective_id=0, has_side_effects=True),
    )(tokens, key_codes, key_exponents.T, key_cotangent, inverse)


def solution(mesh):
    def body(tokens, key_codes, key_exponents, key_cotangent):
        nodes, locals_ = mesh.shape["node"], mesh.shape["local"]
        row_count = tokens.shape[1] // (nodes * locals_)
        grid = nodes == 2 * DEPTH and locals_ == 2 * CORES
        run = fused if grid and row_count % HEAD == 0 else on_device
        return run(tokens, key_codes, key_exponents, key_cotangent)

    return jax.shard_map(
        body,
        mesh=mesh,
        in_specs=(
            P(("node", "local"), None),
            P("local", None),
            P("local", None),
            P(("node", "local"), None),
        ),
        out_specs=(
            P(("node", "local"), None),
            P(("node", "local"), None),
            P(("node", "local"), None),
        ),
        check_vma=False,
    )
```

```python
import functools
import math

import jax
import jax.numpy as jnp
import numpy as np
from jax import lax
from jax.experimental import pallas as pl
from jax.experimental.pallas import tpu as pltpu
from jax.sharding import PartitionSpec as P

KVH = 4
HEAD = 128
QBLOCK = 256
SEQ = 8192
MESH = pl.DeviceIdType.MESH


THETA = 500000.0


def tables(positions):
    inverse = THETA ** (-(jnp.arange(HEAD // 2, dtype=jnp.float32) * 2.0 / HEAD))
    angles = positions.astype(jnp.float32)[:, None] * inverse[None, :]
    return (jnp.cos(angles), jnp.sin(angles))


def rotate(values, cosine, sine_part):
    count = values.shape[0]
    heads = values.reshape(count, KVH, HEAD)
    first_half = heads[:, :, : HEAD // 2]
    second_half = heads[:, :, HEAD // 2 :]
    cos_rows = cosine[:, None, :]
    sin_rows = sine_part[:, None, :]
    joined = jnp.concatenate(
        [
            first_half * cos_rows - second_half * sin_rows,
            second_half * cos_rows + first_half * sin_rows,
        ],
        axis=2,
    )
    return joined.reshape(count, KVH * HEAD)


def unrotate(values, cosine, sine_part):
    count = values.shape[0]
    heads = values.reshape(count, KVH, HEAD)
    first_half = heads[:, :, : HEAD // 2]
    second_half = heads[:, :, HEAD // 2 :]
    cos_rows = cosine[:, None, :]
    sin_rows = sine_part[:, None, :]
    joined = jnp.concatenate(
        [
            first_half * cos_rows + second_half * sin_rows,
            second_half * cos_rows - first_half * sin_rows,
        ],
        axis=2,
    )
    return joined.reshape(count, KVH * HEAD)


def quantize(partial_value):
    blocks = partial_value.reshape(partial_value.shape[0], partial_value.shape[1] // QBLOCK, QBLOCK)
    largest = jnp.max(jnp.abs(blocks), axis=2)
    block_scale = jnp.exp2(jnp.ceil(jnp.log2(largest + 1e-06)))
    code_values = (blocks / block_scale[:, :, None]).astype(jnp.bfloat16)
    return (code_values, block_scale.astype(jnp.bfloat16))


def expand_codes(code_values, block_scale):
    lead = code_values.shape[:-1]
    blocks = code_values.reshape(lead + (block_scale.shape[-1], QBLOCK))
    values = blocks.astype(jnp.float32) * block_scale.astype(jnp.float32)[..., None]
    return values.reshape(lead + (code_values.shape[-1],))


def on_device(tokens, key_codes, key_exponents, key_cotangent):
    node_count = lax.axis_size("node")
    local_count = lax.axis_size("local")
    tok_count = tokens.shape[0]
    width = tokens.shape[1]
    feature_count = key_codes.shape[1]
    expanded = jnp.repeat(jnp.exp2(key_exponents.astype(jnp.float32)), QBLOCK, axis=1)
    shard_weights = (key_codes.astype(jnp.float32) * expanded).astype(jnp.bfloat16)
    weights = lax.all_gather(shard_weights, "local", axis=0, tiled=True)
    device_index = lax.axis_index("node") * local_count + lax.axis_index("local")
    positions = (device_index * tok_count + jnp.arange(tok_count, dtype=jnp.int32)) % SEQ
    cosine, sine_part = tables(positions)
    pre_grad = unrotate(key_cotangent.astype(jnp.float32), cosine, sine_part).astype(jnp.bfloat16)
    partial_value = lax.dot_general(
        tokens, pre_grad, (((0,), (0,)), ((), ())), preferred_element_type=jnp.float32
    )
    code_values, block_scale = quantize(partial_value)
    row_count = width // (node_count * local_count)
    block_count = feature_count // QBLOCK
    code_grid = code_values.reshape(node_count, local_count, row_count, feature_count)
    scale_grid = block_scale.reshape(node_count, local_count, row_count, block_count)
    projected = jnp.dot(tokens, weights, preferred_element_type=jnp.float32)
    keys = rotate(projected, cosine, sine_part).astype(jnp.bfloat16)
    input_grad = lax.dot_general(
        pre_grad, weights, (((1,), (1,)), ((), ())), preferred_element_type=jnp.float32
    ).astype(jnp.bfloat16)
    got_codes, got_scales = (
        lax.all_to_all(code_grid, "local", split_axis=1, concat_axis=1, tiled=True),
        lax.all_to_all(scale_grid, "local", split_axis=1, concat_axis=1, tiled=True),
    )
    node_terms = jnp.sum(expand_codes(got_codes, got_scales), axis=1)
    summed = (
        lax.psum_scatter(node_terms.astype(jnp.bfloat16), "node", scatter_dimension=0, tiled=True)
        .astype(jnp.float32)
        .reshape(row_count, feature_count)
    )
    total_tokens = tok_count * node_count * local_count
    weight_grad = summed * (1.0 / math.sqrt(total_tokens))
    return (keys, input_grad, weight_grad)


def flip(index, distance):
    result = index
    bit = 1
    while bit <= distance:
        if distance & bit:
            result = result + bit - 2 * bit * lax.rem(lax.div(index, bit), 2)
        bit *= 2
    return result


def turn(values, cosine, signed_sine):
    parts = []
    for head in range(values.shape[1] // HEAD):
        piece = values[:, head * HEAD : (head + 1) * HEAD]
        parts.append(piece * cosine + pltpu.roll(piece, HEAD // 2, 1) * signed_sine)
    return jnp.concatenate(parts, axis=1)


CORES = 2
DEPTH = 4
GROUPS = ('S1', 'P2z', 'P2z')
ROUTES = {
    "S1": {
        (0, 0): ("x", {"z": (1, 0), "y": (0, 1)}),
        (1, 0): ("z", {"y": (1, 1)}),
        (0, 1): ("y", {}),
        (1, 1): ("y", {}),
    },
    "S2": {
        (0, 0): ("x", {"y": (0, 1), "z": (1, 0)}),
        (0, 1): ("y", {"z": (1, 1)}),
        (1, 0): ("z", {}),
        (1, 1): ("z", {}),
    },
    "P2z": {(0, 0): ("x", {"z": (1, 0)}), (1, 0): ("z", {})},
    "P2y": {(0, 0): ("x", {"y": (0, 1)}), (0, 1): ("y", {})},
}
SPLIT = 2
PARTS = 2
SIZES = {"S1": 4, "S2": 4, "P2z": 2, "P2y": 2}
ORDER = (
    "exp", "bar", "xw1:00", "yc3f", "xw0:00", "deq", "trg", "ypre",
    "cw", "yc2n", "yc3n", "xw2:00", "w1:00.0", "ccols", "yc2f", "yc1f",
    "cpre", "o3", "o0", "yc1n", "w1:00.1", "yc0f", "w0:00.0", "rpre",
    "w0:00.1", "g3f", "g2n", "w2:00.0", "v0:00", "u1:00", "v1:00", "w1:10.0",
    "w0:10.0", "w2:00.1", "g2f", "g3n", "u0:00", "s00", "g1f", "w0:10.1",
    "p0", "s01", "o2", "u2:00", "v0:10", "w2:10.1", "p1", "s10",
    "yc0n", "g0f", "p2", "g1n", "w1:10.1", "s11", "s20", "w0:01.1",
    "w2:10.0", "u2:10", "w0:01.0", "u0:10", "v1:10", "u0:01", "s21", "u1:10",
    "w0:11.1", "v2:10", "w0:11.0", "p3", "g0n", "o1", "v0:11", "v0:01",
    "u0:11", "v2:00", "key", "fin",
)


def fused_kernel(
    tokens_hbm,
    codes_hbm,
    exponents_hbm,
    cotangent_hbm,
    inverse_hbm,
    keys_ref,
    input_grad_ref,
    weight_grad_ref,
    tokens,
    codes,
    exponents_ref,
    cotangent_ref,
    inverse_ref,
    scale_ref,
    rotation,
    columns,
    pre,
    weights,
    out_x,
    in_x,
    out_z,
    in_z,
    kept,
    projected,
    load_sem,
    own_sem,
    column_send,
    column_recv,
    pre_send,
    pre_recv,
    own_send,
    own_recv,
    weight_send,
    weight_recv,
    sum_send,
    sum_recv,
    line_send,
    line_recv,
):
    node = lax.axis_index("node")
    local = lax.axis_index("local")
    nodes = lax.axis_size("node")
    locals_ = lax.axis_size("local")
    count = tokens.shape[0]
    row_count = columns.shape[2]
    shard_rows = weights.shape[1]
    features = pre.shape[1]
    unit_rows = shard_rows // sum(SIZES[g] for g in GROUPS)
    part_rows = unit_rows // PARTS
    width = features // SPLIT
    total = count * nodes * locals_

    depth_at = lax.div(node, 2)
    inner = lax.div(depth_at * (DEPTH - 1 - depth_at), 2)
    peers = {
        "c": (node, flip(local, 1)),
        "x": (node, flip(local, 2)),
        "y": (flip(node, 1), local),
        "d": (flip(node, 1), flip(local, 1)),
        "z": (flip(node, 2), local),
    }
    neighbours = len(peers)
    barrier = pltpu.get_barrier_semaphore()
    for peer in peers.values():
        pl.semaphore_signal(barrier, inc=1, device_id=peer, device_id_type=MESH)
    peers["m"] = (flip(node, 6), local)

    @pl.when(inner == 1)
    def _():
        pl.semaphore_signal(barrier, inc=1, device_id=peers["m"], device_id_type=MESH)

    def owned(r, far, e=0, d=0):
        first = (flip(node, 2 * r + e) * locals_ + flip(local, 2 * far + d)) * row_count
        return pl.ds(pl.multiple_of(first, row_count), row_count)

    def slot_rows(slot):
        return pl.ds(slot * count, count)

    def lanes_of(k):
        return pl.ds(k * width, width)

    zbit = lax.rem(depth_at, 2)
    ybit = lax.rem(node, 2)
    bases = [sum(SIZES[g] for g in GROUPS[:i]) for i in range(len(GROUPS))]

    def unit_first(group, key):
        kind = GROUPS[group]
        dz, dy = key
        zz = 1 - zbit if dz else zbit
        yy = 1 - ybit if dy else ybit
        index = {"S1": 2 * zz + yy, "S2": 2 * zz + yy, "P2z": zz, "P2y": yy}[kind]
        return pl.multiple_of((bases[group] + index) * unit_rows, unit_rows)

    def sem_index(group, key):
        kind = GROUPS[group]
        dz, dy = key
        return bases[group] + {"S1": 2 * dz + dy, "S2": 2 * dz + dy, "P2z": dz, "P2y": dy}[kind]

    def load(source, target, at):
        copy = pltpu.make_async_copy(source, target, load_sem.at[at])
        copy.start()
        return copy

    load_exponents = load(exponents_hbm, exponents_ref, 0)
    load_codes = {}
    keys = [(g, key) for g in range(len(GROUPS)) for key in ROUTES[GROUPS[g]]]
    first_keys = [(g, key) for g, key in keys if ROUTES[GROUPS[g]][key][0] == "x"]
    rest_keys = [pair for pair in keys if pair not in first_keys]

    def start_codes(pairs):
        for g, key in pairs:
            rows = pl.ds(unit_first(g, key), unit_rows)
            load_codes[g, key] = load(
                codes_hbm.at[rows, :], codes.at[rows, :], 4 + sem_index(g, key)
            )

    start_codes(first_keys)
    load_inverse = load(inverse_hbm, inverse_ref, 1)
    load_cotangent = load(cotangent_hbm, cotangent_ref, 2)
    start_codes(rest_keys)
    load_tokens = load(tokens_hbm, tokens, 3)
    own = {}
    for r in range(DEPTH - 1, -1, -1):
        for far in range(1, -1, -1):
            k = 2 * r + far
            own[k] = pltpu.make_async_copy(
                tokens_hbm.at[:, owned(r, far)], columns.at[k, slot_rows(0), :], own_sem.at[k]
            )
            own[k].start()

    def rotations():
        start = lax.rem((node * locals_ + local) * count, SEQ)
        positions = lax.rem(start + lax.broadcasted_iota(jnp.int32, (count, HEAD), 0), SEQ)
        load_inverse.wait()
        angles = positions.astype(jnp.float32) * inverse_ref[...]
        cosine = jnp.cos(angles)
        sine = jnp.sin(angles)
        lane = lax.broadcasted_iota(jnp.int32, (count, HEAD), 1)
        signed_sine = jnp.where(lane < HEAD // 2, -sine, sine)
        rotation[0] = cosine
        rotation[1] = signed_sine
        load_cotangent.wait()
        pre[slot_rows(0), :] = turn(
            cotangent_ref[...].astype(jnp.float32), cosine, -signed_sine
        ).astype(jnp.bfloat16)

    def scales():
        load_exponents.wait()
        scale = jnp.left_shift(1, exponents_ref[...] + 15).astype(jnp.float32) * (2.0**-15)
        scale_ref[...] = jnp.transpose(jnp.concatenate([scale] * (8 // scale.shape[0]), axis=0))

    def expand(group, key):
        load_codes[group, key].wait()
        rows = pl.ds(unit_first(group, key), unit_rows)
        for block in range(features // QBLOCK):
            lanes = pl.ds(block * QBLOCK, QBLOCK)
            weights[0, rows, lanes] = (
                codes[rows, lanes].astype(jnp.float32) * scale_ref[rows, block : block + 1]
            ).astype(jnp.bfloat16)

    sends = []
    waits = {}

    def describe(src, dst, send_sem, recv_sem, peer):
        return pltpu.make_async_remote_copy(
            src_ref=src,
            dst_ref=dst,
            send_sem=send_sem,
            recv_sem=recv_sem,
            device_id=peers[peer],
            device_id_type=MESH,
        )

    def send(src, dst, send_sem, recv_sem, peer):
        copy = describe(src, dst, send_sem, recv_sem, peer)
        copy.start()
        sends.append(copy)
        return copy

    def send_columns(name, slot, peer, r, far, e, d):
        k = 2 * r + far
        waits[name, k] = send(
            tokens_hbm.at[:, owned(r, far, e, d)],
            columns.at[k, slot_rows(slot), :],
            column_send.at[k, slot],
            column_recv.at[k, slot],
            peer,
        )

    def send_pre(source, slot, peer):
        waits["pre", slot] = send(
            pre.at[slot_rows(source), :],
            pre.at[slot_rows(slot), :],
            pre_send.at[slot],
            pre_recv.at[slot],
            peer,
        )

    blocks = 4
    block_rows = shard_rows // blocks

    def use(slot, first, length):
        rows = pl.ds(pl.multiple_of(first, length), length)
        lane_first = flip(local, slot) * shard_rows + first
        lanes = pl.ds(pl.multiple_of(lane_first, length), length)
        block = weights[slot, rows, :]
        input_grad_ref[:, lanes] = lax.dot_general(
            pre[slot_rows(0), :],
            block,
            (((1,), (1,)), ((), ())),
            preferred_element_type=jnp.float32,
        ).astype(jnp.bfloat16)
        projected[...] += jnp.dot(
            tokens[:, lanes], block, preferred_element_type=jnp.float32
        )

    def send_unit(source, slot, group, source_key, key, part, peer):
        first = unit_first(group, source_key) + part * part_rows
        rows = pl.ds(pl.multiple_of(first, part_rows), part_rows)
        lane_of = {"x": 0, "y": 1, "z": 2, "c": 3}[peer]
        waits["w", slot, group, key, part] = send(
            weights.at[source, rows, :],
            weights.at[slot, rows, :],
            weight_send.at[lane_of, sem_index(group, source_key), part],
            weight_recv.at[slot - 2, sem_index(group, key), part],
            peer,
        )

    def piece(r, far):
        k = 2 * r + far
        own[k].wait()
        for name in "cyd":
            waits[name, k].wait_recv()
        return lax.dot_general(
            columns[k], pre[...], (((0,), (0,)), ((), ())), preferred_element_type=jnp.float32
        )

    line = {}
    for i in range(DEPTH - 1):
        for k in range(SPLIT):
            for middle in range(2):
                slot = i + DEPTH - 1 if middle and i < 2 else i
                line[middle, i, k] = describe(
                    out_z.at[i * SPLIT + k],
                    in_z.at[slot * SPLIT + k],
                    line_send.at[i * SPLIT + k],
                    line_recv.at[slot * SPLIT + k],
                    "m" if middle and i < 2 else "z",
                )
    order_of = ((3, 2, 1), (2, 3, 1))

    def chain(i, k):
        for middle in range(2):

            @pl.when(inner == middle)
            def _():
                r = order_of[middle][i]
                waits["x", r, k].wait_recv()
                value = kept[r, :, lanes_of(k)] + in_x[r * SPLIT + k].astype(jnp.float32)
                if middle:
                    line[0 if i < 2 else 1, i if i < 2 else 0, k].wait_recv()
                    slot = i if i < 2 else DEPTH - 1
                    value = value + in_z[slot * SPLIT + k].astype(jnp.float32)
                out_z[i * SPLIT + k] = value.astype(jnp.bfloat16)
                line[middle, i, k].start()

    gain = 1.0 / math.sqrt(total)

    def finish(k):
        waits["x", 0, k].wait_recv()
        summed = kept[0, :, lanes_of(k)] + in_x[k].astype(jnp.float32)
        line[0, 2, k].wait_recv()
        summed = summed + in_z[2 * SPLIT + k].astype(jnp.float32)
        weight_grad_ref[:, lanes_of(k)] = summed * gain

        @pl.when(inner == 1)
        def _():
            line[1, 1, k].wait_recv()
            last = in_z[DEPTH * SPLIT + k].astype(jnp.float32)
            weight_grad_ref[:, lanes_of(k)] += last * gain

    pre_ready = []

    def run(step):
        head, _, rest = step.partition(":")
        if step == "ypre":
            send_pre(0, 2, "y")
        elif step == "cpre":
            send_pre(0, 1, "c")
        elif step == "exp":
            scales()
            for group, key in first_keys:
                expand(group, key)
        elif step == "trg":
            rotations()
        elif step == "deq":
            for group, key in rest_keys:
                expand(group, key)
            load_tokens.wait()
            projected[...] = jnp.zeros_like(projected)
        elif step == "rpre":
            waits["pre", 2].wait_recv()
            send_pre(2, 3, "c")
        elif step == "ccols":
            for r in (3, 2, 1, 0):
                for far in (1, 0):
                    send_columns("c", 1, "c", r, far, 0, 1)
        elif step == "cw":
            for b in range(blocks):
                rows = pl.ds(b * block_rows, block_rows)
                waits["own", b] = send(
                    weights.at[0, rows, :],
                    weights.at[1, rows, :],
                    own_send.at[b],
                    own_recv.at[b],
                    "c",
                )
        elif head[:2] == "yc":
            r, far = int(head[2]), int(head[3] == "f")
            send_columns("y", 2, "y", r, far, 1, 0)
            send_columns("d", 3, "d", r, far, 1, 1)
        elif head[:2] == "xw":
            group, key = int(head[2:]), (int(rest[0]), int(rest[1]))
            for part in range(PARTS):
                send_unit(0, 2, group, key, key, part, "x")
        elif head[0] == "o":
            use(0, int(head[1]) * block_rows, block_rows)
        elif head[0] == "p":
            waits["own", int(head[1])].wait_recv()
            use(1, int(head[1]) * block_rows, block_rows)
        elif head[0] == "w":
            group, key = int(head[1:]), (int(rest[0]), int(rest[1]))
            part = int(rest[3])
            waits["w", 2, group, key, part].wait_recv()
            for peer, there in ROUTES[GROUPS[group]][key][1].items():
                send_unit(2, 2, group, key, there, part, peer)
            send_unit(2, 3, group, key, key, part, "c")
        elif head[0] in "uv":
            group, key = int(head[1:]), (int(rest[0]), int(rest[1]))
            slot = 2 if head[0] == "u" else 3
            if slot == 3:
                for part in range(PARTS):
                    waits["w", 3, group, key, part].wait_recv()
            use(slot, unit_first(group, key), unit_rows)
        elif head[0] == "g":
            r, far = int(head[1]), int(head[2] == "f")
            if not pre_ready:
                waits["pre", 1].wait_recv()
                waits["pre", 3].wait_recv()
                pre_ready.append(True)
            value = piece(r, far)
            if far:
                for k in range(SPLIT):
                    at = r * SPLIT + k
                    out_x[at] = value[:, k * width : (k + 1) * width].astype(jnp.bfloat16)
                    waits["x", r, k] = send(
                        out_x.at[at], in_x.at[at], sum_send.at[at], sum_recv.at[at], "x"
                    )
            else:
                kept[r] = value
        elif head[0] == "s":
            chain(int(head[1]), int(head[2]))
        elif step == "key":
            keys_ref[...] = turn(projected[...], rotation[0], rotation[1]).astype(jnp.bfloat16)
        elif step == "fin":
            for k in range(SPLIT):
                finish(k)
        elif step == "bar":
            pl.semaphore_wait(barrier, neighbours + inner)
        else:
            raise ValueError(step)

    steps = ORDER
    if "bar" not in steps:
        run("bar")
    for step in steps:
        run(step)
    for copy in sends:
        copy.wait_send()
    for middle in range(2):

        @pl.when(inner == middle)
        def _():
            for i in range(DEPTH - 1):
                for k in range(SPLIT):
                    line[middle, i, k].wait_send()


def place(*refs):
    copies = [pltpu.make_async_copy(refs[i], refs[3 + i], refs[6].at[i]) for i in range(3)]
    for copy in copies:
        copy.start()
    for copy in copies:
        copy.wait()


def fused(tokens, key_codes, key_exponents, key_cotangent):
    nodes = lax.axis_size("node")
    locals_ = lax.axis_size("local")
    count, width = tokens.shape
    shard_rows, features = key_codes.shape
    row_count = width // (nodes * locals_)
    units = sum(SIZES[g] for g in GROUPS)
    half = THETA ** (-(np.arange(HEAD // 2) * 2.0 / HEAD))
    inverse = jnp.asarray(np.concatenate([half, half])[None, :], jnp.float32)
    anywhere = pl.BlockSpec(memory_space=pl.ANY)
    vmem = pl.BlockSpec(memory_space=pltpu.VMEM)
    dma = pltpu.SemaphoreType.DMA
    held = pl.pallas_call(
        fused_kernel,
        out_shape=(
            pltpu.VMEM((count, features), jnp.bfloat16),
            pltpu.VMEM((count, width), jnp.bfloat16),
            pltpu.VMEM((row_count, features), jnp.float32),
        ),
        in_specs=[anywhere] * 5,
        out_specs=(vmem, vmem, vmem),
        scratch_shapes=[
            pltpu.VMEM((count, width), jnp.bfloat16),
            pltpu.VMEM((shard_rows, features), jnp.bfloat16),
            pltpu.VMEM(key_exponents.shape[::-1], jnp.int32),
            pltpu.VMEM((count, features), jnp.bfloat16),
            pltpu.VMEM((1, HEAD), jnp.float32),
            pltpu.VMEM((shard_rows, 8), jnp.float32),
            pltpu.VMEM((2, count, HEAD), jnp.float32),
            pltpu.VMEM((2 * DEPTH, locals_ * count, row_count), jnp.bfloat16),
            pltpu.VMEM((locals_ * count, features), jnp.bfloat16),
            pltpu.VMEM((locals_, shard_rows, features), jnp.bfloat16),
            pltpu.VMEM((DEPTH * SPLIT, row_count, features // SPLIT), jnp.bfloat16),
            pltpu.VMEM((DEPTH * SPLIT, row_count, features // SPLIT), jnp.bfloat16),
            pltpu.VMEM((3 * SPLIT, row_count, features // SPLIT), jnp.bfloat16),
            pltpu.VMEM((5 * SPLIT, row_count, features // SPLIT), jnp.bfloat16),
            pltpu.VMEM((DEPTH, row_count, features), jnp.float32),
            pltpu.VMEM((count, features), jnp.float32),
            dma((4 + units,)),
            dma((2 * DEPTH,)),
            dma((2 * DEPTH, 4)),
            dma((2 * DEPTH, 4)),
            dma((4,)),
            dma((4,)),
            dma((4,)),
            dma((4,)),
            dma((4, units, PARTS)),
            dma((2, units, PARTS)),
            dma((DEPTH * SPLIT,)),
            dma((DEPTH * SPLIT,)),
            dma((3 * SPLIT,)),
            dma((5 * SPLIT,)),
        ],
        compiler_params=pltpu.CompilerParams(collective_id=0, has_side_effects=True),
    )(tokens, key_codes, key_exponents.T, key_cotangent, inverse)
    return pl.pallas_call(
        place,
        out_shape=tuple(jax.ShapeDtypeStruct(a.shape, a.dtype) for a in held),
        in_specs=[vmem] * 3,
        out_specs=(anywhere,) * 3,
        scratch_shapes=[dma((3,))],
    )(*(pltpu.with_memory_space_constraint(a, pltpu.VMEM) for a in held))


def solution(mesh):
    def body(tokens, key_codes, key_exponents, key_cotangent):
        nodes, locals_ = mesh.shape["node"], mesh.shape["local"]
        row_count = tokens.shape[1] // (nodes * locals_)
        grid = nodes == 2 * DEPTH and locals_ == 2 * CORES
        run = fused if grid and row_count % HEAD == 0 else on_device
        return run(tokens, key_codes, key_exponents, key_cotangent)

    return jax.shard_map(
        body,
        mesh=mesh,
        in_specs=(
            P(("node", "local"), None),
            P("local", None),
            P("local", None),
            P(("node", "local"), None),
        ),
        out_specs=(
            P(("node", "local"), None),
            P(("node", "local"), None),
            P(("node", "local"), None),
        ),
        check_vma=False,
    )
```

```python
import functools
import math

import jax
import jax.numpy as jnp
import numpy as np
from jax import lax
from jax.experimental import pallas as pl
from jax.experimental.pallas import tpu as pltpu
from jax.sharding import PartitionSpec as P

KVH = 4
HEAD = 128
QBLOCK = 256
SEQ = 8192
MESH = pl.DeviceIdType.MESH


THETA = 500000.0


def tables(positions):
    inverse = THETA ** (-(jnp.arange(HEAD // 2, dtype=jnp.float32) * 2.0 / HEAD))
    angles = positions.astype(jnp.float32)[:, None] * inverse[None, :]
    return (jnp.cos(angles), jnp.sin(angles))


def rotate(values, cosine, sine_part):
    count = values.shape[0]
    heads = values.reshape(count, KVH, HEAD)
    first_half = heads[:, :, : HEAD // 2]
    second_half = heads[:, :, HEAD // 2 :]
    cos_rows = cosine[:, None, :]
    sin_rows = sine_part[:, None, :]
    joined = jnp.concatenate(
        [
            first_half * cos_rows - second_half * sin_rows,
            second_half * cos_rows + first_half * sin_rows,
        ],
        axis=2,
    )
    return joined.reshape(count, KVH * HEAD)


def unrotate(values, cosine, sine_part):
    count = values.shape[0]
    heads = values.reshape(count, KVH, HEAD)
    first_half = heads[:, :, : HEAD // 2]
    second_half = heads[:, :, HEAD // 2 :]
    cos_rows = cosine[:, None, :]
    sin_rows = sine_part[:, None, :]
    joined = jnp.concatenate(
        [
            first_half * cos_rows + second_half * sin_rows,
            second_half * cos_rows - first_half * sin_rows,
        ],
        axis=2,
    )
    return joined.reshape(count, KVH * HEAD)


def quantize(partial_value):
    blocks = partial_value.reshape(partial_value.shape[0], partial_value.shape[1] // QBLOCK, QBLOCK)
    largest = jnp.max(jnp.abs(blocks), axis=2)
    block_scale = jnp.exp2(jnp.ceil(jnp.log2(largest + 1e-06)))
    code_values = (blocks / block_scale[:, :, None]).astype(jnp.bfloat16)
    return (code_values, block_scale.astype(jnp.bfloat16))


def expand_codes(code_values, block_scale):
    lead = code_values.shape[:-1]
    blocks = code_values.reshape(lead + (block_scale.shape[-1], QBLOCK))
    values = blocks.astype(jnp.float32) * block_scale.astype(jnp.float32)[..., None]
    return values.reshape(lead + (code_values.shape[-1],))


def on_device(tokens, key_codes, key_exponents, key_cotangent):
    node_count = lax.axis_size("node")
    local_count = lax.axis_size("local")
    tok_count = tokens.shape[0]
    width = tokens.shape[1]
    feature_count = key_codes.shape[1]
    expanded = jnp.repeat(jnp.exp2(key_exponents.astype(jnp.float32)), QBLOCK, axis=1)
    shard_weights = (key_codes.astype(jnp.float32) * expanded).astype(jnp.bfloat16)
    weights = lax.all_gather(shard_weights, "local", axis=0, tiled=True)
    device_index = lax.axis_index("node") * local_count + lax.axis_index("local")
    positions = (device_index * tok_count + jnp.arange(tok_count, dtype=jnp.int32)) % SEQ
    cosine, sine_part = tables(positions)
    pre_grad = unrotate(key_cotangent.astype(jnp.float32), cosine, sine_part).astype(jnp.bfloat16)
    partial_value = lax.dot_general(
        tokens, pre_grad, (((0,), (0,)), ((), ())), preferred_element_type=jnp.float32
    )
    code_values, block_scale = quantize(partial_value)
    row_count = width // (node_count * local_count)
    block_count = feature_count // QBLOCK
    code_grid = code_values.reshape(node_count, local_count, row_count, feature_count)
    scale_grid = block_scale.reshape(node_count, local_count, row_count, block_count)
    projected = jnp.dot(tokens, weights, preferred_element_type=jnp.float32)
    keys = rotate(projected, cosine, sine_part).astype(jnp.bfloat16)
    input_grad = lax.dot_general(
        pre_grad, weights, (((1,), (1,)), ((), ())), preferred_element_type=jnp.float32
    ).astype(jnp.bfloat16)
    got_codes, got_scales = (
        lax.all_to_all(code_grid, "local", split_axis=1, concat_axis=1, tiled=True),
        lax.all_to_all(scale_grid, "local", split_axis=1, concat_axis=1, tiled=True),
    )
    node_terms = jnp.sum(expand_codes(got_codes, got_scales), axis=1)
    summed = (
        lax.psum_scatter(node_terms.astype(jnp.bfloat16), "node", scatter_dimension=0, tiled=True)
        .astype(jnp.float32)
        .reshape(row_count, feature_count)
    )
    total_tokens = tok_count * node_count * local_count
    weight_grad = summed * (1.0 / math.sqrt(total_tokens))
    return (keys, input_grad, weight_grad)


def flip(index, distance):
    result = index
    bit = 1
    while bit <= distance:
        if distance & bit:
            result = result + bit - 2 * bit * lax.rem(lax.div(index, bit), 2)
        bit *= 2
    return result


def turn(values, cosine, signed_sine):
    parts = []
    for head in range(values.shape[1] // HEAD):
        piece = values[:, head * HEAD : (head + 1) * HEAD]
        parts.append(piece * cosine + pltpu.roll(piece, HEAD // 2, 1) * signed_sine)
    return jnp.concatenate(parts, axis=1)


CORES = 2
DEPTH = 4
GROUPS = (('S1', 'S1'), ('Q2z', 'Q2z'))
OVER = ()
ROUTES = {
    "S1": {
        (0, 0): ("x", {"z": (1, 0), "y": (0, 1)}),
        (1, 0): ("z", {"y": (1, 1)}),
        (0, 1): ("y", {}),
        (1, 1): ("y", {}),
    },
    "S2": {
        (0, 0): ("x", {"y": (0, 1), "z": (1, 0)}),
        (0, 1): ("y", {"z": (1, 1)}),
        (1, 0): ("z", {}),
        (1, 1): ("z", {}),
    },
    "Q2z": {
        (0, 0): ("x", {"z": (1, 0)}),
        (0, 1): ("x", {"z": (1, 1)}),
        (1, 0): ("z", {}),
        (1, 1): ("z", {}),
    },
    "Q2y": {
        (0, 0): ("x", {"y": (0, 1)}),
        (1, 0): ("x", {"y": (1, 1)}),
        (0, 1): ("y", {}),
        (1, 1): ("y", {}),
    },
}
KEYS = ((0, 0), (0, 1), (1, 0), (1, 1))
SPLIT = 2
PARTS = len(GROUPS[0])
ORDER = (
    "exp", "bar", "yc3f", "xw1:01.0", "xw0:00.0", "xw1:01.1", "trg", "ypre",
    "yc2f", "deq", "xw1:00.1", "ccols", "w1:01.0", "yc3n", "yc2n", "w0:00.0",
    "xw0:00.1", "cpre", "yc1f", "rpre", "w1:01.1", "yc0f", "g3f", "xw1:00.0",
    "yc1n", "cw", "w1:00.1", "o2", "w0:00.1", "g2f", "p0", "g3n",
    "w0:10.0", "g2n", "s00e", "u0:00", "s01e", "p1", "g1f", "w1:11.0",
    "w0:10.1", "w1:10.1", "s00i", "o0", "w1:00.0", "s10e", "v1:01", "o1",
    "yc0n", "s01i", "g0f", "s11e", "w0:01.0", "g1n", "u1:00", "u1:01",
    "p3", "s20e", "s10i", "s20i", "w1:11.1", "s11i", "s21i", "w1:10.0",
    "s21e", "o3", "w0:11.0", "u1:10", "p2", "w0:01.1", "w0:11.1", "v0:10",
    "u1:11", "g0n", "v0:00", "u0:11", "v1:10", "u0:01", "v1:00", "u0:10",
    "v0:11", "v0:01", "v1:11", "key", "fin",
)


def fused_kernel(
    tokens_hbm,
    codes_hbm,
    exponents_hbm,
    cotangent_hbm,
    inverse_hbm,
    keys_ref,
    input_grad_ref,
    weight_grad_ref,
    tokens,
    codes,
    exponents_ref,
    cotangent_ref,
    inverse_ref,
    scale_ref,
    rotation,
    columns,
    pre,
    weights,
    out_x,
    in_x,
    out_z,
    in_z,
    kept,
    projected,
    load_sem,
    own_sem,
    column_send,
    column_recv,
    pre_send,
    pre_recv,
    own_send,
    own_recv,
    weight_send,
    weight_recv,
    sum_send,
    sum_recv,
    line_send,
    line_recv,
):
    node = lax.axis_index("node")
    local = lax.axis_index("local")
    nodes = lax.axis_size("node")
    locals_ = lax.axis_size("local")
    count = tokens.shape[0]
    row_count = columns.shape[2]
    shard_rows = weights.shape[1]
    features = pre.shape[1]
    unit_rows = shard_rows // (len(KEYS) * len(GROUPS))
    part_rows = unit_rows // PARTS
    width = features // SPLIT
    total = count * nodes * locals_

    depth_at = lax.div(node, 2)
    inner = lax.div(depth_at * (DEPTH - 1 - depth_at), 2)
    peers = {
        "c": (node, flip(local, 1)),
        "x": (node, flip(local, 2)),
        "y": (flip(node, 1), local),
        "d": (flip(node, 1), flip(local, 1)),
        "z": (flip(node, 2), local),
    }
    neighbours = len(peers)
    barrier = pltpu.get_barrier_semaphore()
    for peer in peers.values():
        pl.semaphore_signal(barrier, inc=1, device_id=peer, device_id_type=MESH)
    peers["m"] = (flip(node, 6), local)

    @pl.when(inner == 1)
    def _():
        pl.semaphore_signal(barrier, inc=1, device_id=peers["m"], device_id_type=MESH)

    def owned(r, far, e=0, d=0):
        first = (flip(node, 2 * r + e) * locals_ + flip(local, 2 * far + d)) * row_count
        return pl.ds(pl.multiple_of(first, row_count), row_count)

    def slot_rows(slot):
        return pl.ds(slot * count, count)

    def lanes_of(k):
        return pl.ds(k * width, width)

    zbit = lax.rem(depth_at, 2)
    ybit = lax.rem(node, 2)

    def unit_first(group, key):
        zz = 1 - zbit if key[0] else zbit
        yy = 1 - ybit if key[1] else ybit
        return pl.multiple_of((len(KEYS) * group + 2 * zz + yy) * unit_rows, unit_rows)

    def sem_index(group, key):
        return len(KEYS) * group + 2 * key[0] + key[1]

    def load(source, target, at):
        copy = pltpu.make_async_copy(source, target, load_sem.at[at])
        copy.start()
        return copy

    load_exponents = load(exponents_hbm, exponents_ref, 0)
    load_codes = {}
    keys = [(g, key) for g in range(len(GROUPS)) for key in KEYS]
    first_keys = [
        (g, key) for g, key in keys if any(ROUTES[kind][key][0] == "x" for kind in GROUPS[g])
    ]
    rest_keys = [pair for pair in keys if pair not in first_keys]

    def start_codes(pairs):
        for g, key in pairs:
            rows = pl.ds(unit_first(g, key), unit_rows)
            load_codes[g, key] = load(
                codes_hbm.at[rows, :], codes.at[rows, :], 4 + sem_index(g, key)
            )

    start_codes(first_keys)
    load_inverse = load(inverse_hbm, inverse_ref, 1)
    load_cotangent = load(cotangent_hbm, cotangent_ref, 2)
    start_codes(rest_keys)
    load_tokens = load(tokens_hbm, tokens, 3)
    own = {}
    for r in range(DEPTH - 1, -1, -1):
        for far in range(1, -1, -1):
            k = 2 * r + far
            own[k] = pltpu.make_async_copy(
                tokens_hbm.at[:, owned(r, far)], columns.at[k, slot_rows(0), :], own_sem.at[k]
            )
            own[k].start()

    def rotations():
        start = lax.rem((node * locals_ + local) * count, SEQ)
        positions = lax.rem(start + lax.broadcasted_iota(jnp.int32, (count, HEAD), 0), SEQ)
        load_inverse.wait()
        angles = positions.astype(jnp.float32) * inverse_ref[...]
        cosine = jnp.cos(angles)
        sine = jnp.sin(angles)
        lane = lax.broadcasted_iota(jnp.int32, (count, HEAD), 1)
        signed_sine = jnp.where(lane < HEAD // 2, -sine, sine)
        rotation[0] = cosine
        rotation[1] = signed_sine
        load_cotangent.wait()
        pre[slot_rows(0), :] = turn(
            cotangent_ref[...].astype(jnp.float32), cosine, -signed_sine
        ).astype(jnp.bfloat16)

    def scales():
        load_exponents.wait()
        scale = jnp.left_shift(1, exponents_ref[...] + 15).astype(jnp.float32) * (2.0**-15)
        scale_ref[...] = jnp.transpose(jnp.concatenate([scale] * (8 // scale.shape[0]), axis=0))

    def expand(group, key):
        load_codes[group, key].wait()
        rows = pl.ds(unit_first(group, key), unit_rows)
        for block in range(features // QBLOCK):
            lanes = pl.ds(block * QBLOCK, QBLOCK)
            weights[0, rows, lanes] = (
                codes[rows, lanes].astype(jnp.float32) * scale_ref[rows, block : block + 1]
            ).astype(jnp.bfloat16)

    sends = []
    waits = {}

    def describe(src, dst, send_sem, recv_sem, peer):
        return pltpu.make_async_remote_copy(
            src_ref=src,
            dst_ref=dst,
            send_sem=send_sem,
            recv_sem=recv_sem,
            device_id=peers[peer],
            device_id_type=MESH,
        )

    inner_sends = []

    def send(src, dst, send_sem, recv_sem, peer, only=None):
        copy = describe(src, dst, send_sem, recv_sem, peer)
        if only is None:
            copy.start()
            sends.append(copy)
        else:
            only.append(copy)

            @pl.when(inner == 1)
            def _():
                copy.start()

        return copy

    def send_columns(name, slot, peer, r, far, e, d):
        k = 2 * r + far
        waits[name, k] = send(
            tokens_hbm.at[:, owned(r, far, e, d)],
            columns.at[k, slot_rows(slot), :],
            column_send.at[k, slot],
            column_recv.at[k, slot],
            peer,
        )

    def send_pre(source, slot, peer):
        waits["pre", slot] = send(
            pre.at[slot_rows(source), :],
            pre.at[slot_rows(slot), :],
            pre_send.at[slot],
            pre_recv.at[slot],
            peer,
        )

    blocks = 4
    block_rows = shard_rows // blocks

    def use(slot, first, length):
        rows = pl.ds(pl.multiple_of(first, length), length)
        lane_first = flip(local, slot) * shard_rows + first
        lanes = pl.ds(pl.multiple_of(lane_first, length), length)
        block = weights[slot, rows, :]
        input_grad_ref[:, lanes] = lax.dot_general(
            pre[slot_rows(0), :],
            block,
            (((1,), (1,)), ((), ())),
            preferred_element_type=jnp.float32,
        ).astype(jnp.bfloat16)
        projected[...] += jnp.dot(
            tokens[:, lanes], block, preferred_element_type=jnp.float32
        )

    def send_unit(source, slot, group, source_key, key, part, peer):
        first = unit_first(group, source_key) + part * part_rows
        rows = pl.ds(pl.multiple_of(first, part_rows), part_rows)
        lane_of = {"x": 0, "y": 1, "z": 2, "c": 3, "m": 4}[peer]
        only = inner_sends if peer in "zm" and (group, part, source_key) in OVER else None
        waits["w", slot, group, key, part] = send(
            weights.at[source, rows, :],
            weights.at[slot, rows, :],
            weight_send.at[lane_of, sem_index(group, source_key), part],
            weight_recv.at[slot - 2, sem_index(group, key), part],
            peer,
            only,
        )

    def piece(r, far):
        k = 2 * r + far
        own[k].wait()
        for name in "cyd":
            waits[name, k].wait_recv()
        return lax.dot_general(
            columns[k], pre[...], (((0,), (0,)), ((), ())), preferred_element_type=jnp.float32
        )

    line = {}
    for i in range(DEPTH - 1):
        for k in range(SPLIT):
            for middle in range(2):
                slot = i + DEPTH - 1 if middle and i < 2 else i
                line[middle, i, k] = describe(
                    out_z.at[i * SPLIT + k],
                    in_z.at[slot * SPLIT + k],
                    line_send.at[i * SPLIT + k],
                    line_recv.at[slot * SPLIT + k],
                    "m" if middle and i < 2 else "z",
                )
    order_of = ((3, 2, 1), (2, 3, 1))

    def chain(i, k, places):
        for middle in places:

            @pl.when(inner == middle)
            def _():
                r = order_of[middle][i]
                waits["x", r, k].wait_recv()
                value = kept[r, :, lanes_of(k)] + in_x[r * SPLIT + k].astype(jnp.float32)
                if middle:
                    line[0 if i < 2 else 1, i if i < 2 else 0, k].wait_recv()
                    slot = i if i < 2 else DEPTH - 1
                    value = value + in_z[slot * SPLIT + k].astype(jnp.float32)
                out_z[i * SPLIT + k] = value.astype(jnp.bfloat16)
                line[middle, i, k].start()

    gain = 1.0 / math.sqrt(total)

    def finish(k):
        waits["x", 0, k].wait_recv()
        summed = kept[0, :, lanes_of(k)] + in_x[k].astype(jnp.float32)
        line[0, 2, k].wait_recv()
        summed = summed + in_z[2 * SPLIT + k].astype(jnp.float32)
        weight_grad_ref[:, lanes_of(k)] = summed * gain

        @pl.when(inner == 1)
        def _():
            line[1, 1, k].wait_recv()
            last = in_z[DEPTH * SPLIT + k].astype(jnp.float32)
            weight_grad_ref[:, lanes_of(k)] += last * gain

    pre_ready = []

    def run(step):
        head, _, rest = step.partition(":")
        if step == "ypre":
            send_pre(0, 2, "y")
        elif step == "cpre":
            send_pre(0, 1, "c")
        elif step == "exp":
            scales()
            for group, key in first_keys:
                expand(group, key)
        elif step == "trg":
            rotations()
        elif step == "deq":
            for group, key in rest_keys:
                expand(group, key)
            load_tokens.wait()
            projected[...] = jnp.zeros_like(projected)
        elif step == "rpre":
            waits["pre", 2].wait_recv()
            send_pre(2, 3, "c")
        elif step == "ccols":
            for r in (3, 2, 1, 0):
                for far in (1, 0):
                    send_columns("c", 1, "c", r, far, 0, 1)
        elif step == "cw":
            for b in range(blocks):
                rows = pl.ds(b * block_rows, block_rows)
                waits["own", b] = send(
                    weights.at[0, rows, :],
                    weights.at[1, rows, :],
                    own_send.at[b],
                    own_recv.at[b],
                    "c",
                )
        elif head[:2] == "yc":
            r, far = int(head[2]), int(head[3] == "f")
            send_columns("y", 2, "y", r, far, 1, 0)
            send_columns("d", 3, "d", r, far, 1, 1)
        elif head[:2] == "xw":
            group, key = int(head[2:]), (int(rest[0]), int(rest[1]))
            send_unit(0, 2, group, key, key, int(rest[3]), "x")
        elif head[0] == "o":
            use(0, int(head[1]) * block_rows, block_rows)
        elif head[0] == "p":
            waits["own", int(head[1])].wait_recv()
            use(1, int(head[1]) * block_rows, block_rows)
        elif head[0] == "w":
            group, key = int(head[1:]), (int(rest[0]), int(rest[1]))
            part = int(rest[3])
            waits["w", 2, group, key, part].wait_recv()
            for peer, there in ROUTES[GROUPS[group][part]][key][1].items():
                send_unit(2, 2, group, key, there, part, peer)
                if peer == "z" and (group, part, key) in OVER:
                    send_unit(2, 2, group, key, there, part, "m")
            send_unit(2, 3, group, key, key, part, "c")
        elif head[0] in "uv":
            group, key = int(head[1:]), (int(rest[0]), int(rest[1]))
            slot = 2 if head[0] == "u" else 3
            if slot == 3:
                for part in range(PARTS):
                    waits["w", 3, group, key, part].wait_recv()
            use(slot, unit_first(group, key), unit_rows)
        elif head[0] == "g":
            r, far = int(head[1]), int(head[2] == "f")
            if not pre_ready:
                waits["pre", 1].wait_recv()
                waits["pre", 3].wait_recv()
                pre_ready.append(True)
            value = piece(r, far)
            if far:
                for k in range(SPLIT):
                    at = r * SPLIT + k
                    out_x[at] = value[:, k * width : (k + 1) * width].astype(jnp.bfloat16)
                    waits["x", r, k] = send(
                        out_x.at[at], in_x.at[at], sum_send.at[at], sum_recv.at[at], "x"
                    )
            else:
                kept[r] = value
        elif head[0] == "s":
            chain(int(head[1]), int(head[2]), ("ei".index(head[3]),))
        elif step == "key":
            keys_ref[...] = turn(projected[...], rotation[0], rotation[1]).astype(jnp.bfloat16)
        elif step == "fin":
            for k in range(SPLIT):
                finish(k)
        elif step == "bar":
            pl.semaphore_wait(barrier, neighbours + inner)
        else:
            raise ValueError(step)

    steps = ORDER
    if "bar" not in steps:
        run("bar")
    for step in steps:
        run(step)
    for copy in sends:
        copy.wait_send()

    @pl.when(inner == 1)
    def _():
        for copy in inner_sends:
            copy.wait_send()

    for middle in range(2):

        @pl.when(inner == middle)
        def _():
            for i in range(DEPTH - 1):
                for k in range(SPLIT):
                    line[middle, i, k].wait_send()


def place(*refs):
    copies = [pltpu.make_async_copy(refs[i], refs[3 + i], refs[6].at[i]) for i in range(3)]
    for copy in copies:
        copy.start()
    for copy in copies:
        copy.wait()


def fused(tokens, key_codes, key_exponents, key_cotangent):
    nodes = lax.axis_size("node")
    locals_ = lax.axis_size("local")
    count, width = tokens.shape
    shard_rows, features = key_codes.shape
    row_count = width // (nodes * locals_)
    units = len(KEYS) * len(GROUPS)
    half = THETA ** (-(np.arange(HEAD // 2) * 2.0 / HEAD))
    inverse = jnp.asarray(np.concatenate([half, half])[None, :], jnp.float32)
    anywhere = pl.BlockSpec(memory_space=pl.ANY)
    vmem = pl.BlockSpec(memory_space=pltpu.VMEM)
    dma = pltpu.SemaphoreType.DMA
    held = pl.pallas_call(
        fused_kernel,
        out_shape=(
            pltpu.VMEM((count, features), jnp.bfloat16),
            pltpu.VMEM((count, width), jnp.bfloat16),
            pltpu.VMEM((row_count, features), jnp.float32),
        ),
        in_specs=[anywhere] * 5,
        out_specs=(vmem, vmem, vmem),
        scratch_shapes=[
            pltpu.VMEM((count, width), jnp.bfloat16),
            pltpu.VMEM((shard_rows, features), jnp.bfloat16),
            pltpu.VMEM(key_exponents.shape[::-1], jnp.int32),
            pltpu.VMEM((count, features), jnp.bfloat16),
            pltpu.VMEM((1, HEAD), jnp.float32),
            pltpu.VMEM((shard_rows, 8), jnp.float32),
            pltpu.VMEM((2, count, HEAD), jnp.float32),
            pltpu.VMEM((2 * DEPTH, locals_ * count, row_count), jnp.bfloat16),
            pltpu.VMEM((locals_ * count, features), jnp.bfloat16),
            pltpu.VMEM((locals_, shard_rows, features), jnp.bfloat16),
            pltpu.VMEM((DEPTH * SPLIT, row_count, features // SPLIT), jnp.bfloat16),
            pltpu.VMEM((DEPTH * SPLIT, row_count, features // SPLIT), jnp.bfloat16),
            pltpu.VMEM((3 * SPLIT, row_count, features // SPLIT), jnp.bfloat16),
            pltpu.VMEM((5 * SPLIT, row_count, features // SPLIT), jnp.bfloat16),
            pltpu.VMEM((DEPTH, row_count, features), jnp.float32),
            pltpu.VMEM((count, features), jnp.float32),
            dma((4 + units,)),
            dma((2 * DEPTH,)),
            dma((2 * DEPTH, 4)),
            dma((2 * DEPTH, 4)),
            dma((4,)),
            dma((4,)),
            dma((4,)),
            dma((4,)),
            dma((5, units, PARTS)),
            dma((2, units, PARTS)),
            dma((DEPTH * SPLIT,)),
            dma((DEPTH * SPLIT,)),
            dma((3 * SPLIT,)),
            dma((5 * SPLIT,)),
        ],
        compiler_params=pltpu.CompilerParams(collective_id=0, has_side_effects=True),
    )(tokens, key_codes, key_exponents.T, key_cotangent, inverse)
    return pl.pallas_call(
        place,
        out_shape=tuple(jax.ShapeDtypeStruct(a.shape, a.dtype) for a in held),
        in_specs=[vmem] * 3,
        out_specs=(anywhere,) * 3,
        scratch_shapes=[dma((3,))],
    )(*(pltpu.with_memory_space_constraint(a, pltpu.VMEM) for a in held))


def solution(mesh):
    def body(tokens, key_codes, key_exponents, key_cotangent):
        nodes, locals_ = mesh.shape["node"], mesh.shape["local"]
        row_count = tokens.shape[1] // (nodes * locals_)
        grid = nodes == 2 * DEPTH and locals_ == 2 * CORES
        run = fused if grid and row_count % HEAD == 0 else on_device
        return run(tokens, key_codes, key_exponents, key_cotangent)

    return jax.shard_map(
        body,
        mesh=mesh,
        in_specs=(
            P(("node", "local"), None),
            P("local", None),
            P("local", None),
            P(("node", "local"), None),
        ),
        out_specs=(
            P(("node", "local"), None),
            P(("node", "local"), None),
            P(("node", "local"), None),
        ),
        check_vma=False,
    )
```

```python
import functools
import math

import jax
import jax.numpy as jnp
import numpy as np
from jax import lax
from jax.experimental import pallas as pl
from jax.experimental.pallas import tpu as pltpu
from jax.sharding import PartitionSpec as P

KVH = 4
HEAD = 128
QBLOCK = 256
SEQ = 8192
MESH = pl.DeviceIdType.MESH


THETA = 500000.0


def tables(positions):
    inverse = THETA ** (-(jnp.arange(HEAD // 2, dtype=jnp.float32) * 2.0 / HEAD))
    angles = positions.astype(jnp.float32)[:, None] * inverse[None, :]
    return (jnp.cos(angles), jnp.sin(angles))


def rotate(values, cosine, sine_part):
    count = values.shape[0]
    heads = values.reshape(count, KVH, HEAD)
    first_half = heads[:, :, : HEAD // 2]
    second_half = heads[:, :, HEAD // 2 :]
    cos_rows = cosine[:, None, :]
    sin_rows = sine_part[:, None, :]
    joined = jnp.concatenate(
        [
            first_half * cos_rows - second_half * sin_rows,
            second_half * cos_rows + first_half * sin_rows,
        ],
        axis=2,
    )
    return joined.reshape(count, KVH * HEAD)


def unrotate(values, cosine, sine_part):
    count = values.shape[0]
    heads = values.reshape(count, KVH, HEAD)
    first_half = heads[:, :, : HEAD // 2]
    second_half = heads[:, :, HEAD // 2 :]
    cos_rows = cosine[:, None, :]
    sin_rows = sine_part[:, None, :]
    joined = jnp.concatenate(
        [
            first_half * cos_rows + second_half * sin_rows,
            second_half * cos_rows - first_half * sin_rows,
        ],
        axis=2,
    )
    return joined.reshape(count, KVH * HEAD)


def quantize(partial_value):
    blocks = partial_value.reshape(partial_value.shape[0], partial_value.shape[1] // QBLOCK, QBLOCK)
    largest = jnp.max(jnp.abs(blocks), axis=2)
    block_scale = jnp.exp2(jnp.ceil(jnp.log2(largest + 1e-06)))
    code_values = (blocks / block_scale[:, :, None]).astype(jnp.bfloat16)
    return (code_values, block_scale.astype(jnp.bfloat16))


def expand_codes(code_values, block_scale):
    lead = code_values.shape[:-1]
    blocks = code_values.reshape(lead + (block_scale.shape[-1], QBLOCK))
    values = blocks.astype(jnp.float32) * block_scale.astype(jnp.float32)[..., None]
    return values.reshape(lead + (code_values.shape[-1],))


def on_device(tokens, key_codes, key_exponents, key_cotangent):
    node_count = lax.axis_size("node")
    local_count = lax.axis_size("local")
    tok_count = tokens.shape[0]
    width = tokens.shape[1]
    feature_count = key_codes.shape[1]
    expanded = jnp.repeat(jnp.exp2(key_exponents.astype(jnp.float32)), QBLOCK, axis=1)
    shard_weights = (key_codes.astype(jnp.float32) * expanded).astype(jnp.bfloat16)
    weights = lax.all_gather(shard_weights, "local", axis=0, tiled=True)
    device_index = lax.axis_index("node") * local_count + lax.axis_index("local")
    positions = (device_index * tok_count + jnp.arange(tok_count, dtype=jnp.int32)) % SEQ
    cosine, sine_part = tables(positions)
    pre_grad = unrotate(key_cotangent.astype(jnp.float32), cosine, sine_part).astype(jnp.bfloat16)
    partial_value = lax.dot_general(
        tokens, pre_grad, (((0,), (0,)), ((), ())), preferred_element_type=jnp.float32
    )
    code_values, block_scale = quantize(partial_value)
    row_count = width // (node_count * local_count)
    block_count = feature_count // QBLOCK
    code_grid = code_values.reshape(node_count, local_count, row_count, feature_count)
    scale_grid = block_scale.reshape(node_count, local_count, row_count, block_count)
    projected = jnp.dot(tokens, weights, preferred_element_type=jnp.float32)
    keys = rotate(projected, cosine, sine_part).astype(jnp.bfloat16)
    input_grad = lax.dot_general(
        pre_grad, weights, (((1,), (1,)), ((), ())), preferred_element_type=jnp.float32
    ).astype(jnp.bfloat16)
    got_codes, got_scales = (
        lax.all_to_all(code_grid, "local", split_axis=1, concat_axis=1, tiled=True),
        lax.all_to_all(scale_grid, "local", split_axis=1, concat_axis=1, tiled=True),
    )
    node_terms = jnp.sum(expand_codes(got_codes, got_scales), axis=1)
    summed = (
        lax.psum_scatter(node_terms.astype(jnp.bfloat16), "node", scatter_dimension=0, tiled=True)
        .astype(jnp.float32)
        .reshape(row_count, feature_count)
    )
    total_tokens = tok_count * node_count * local_count
    weight_grad = summed * (1.0 / math.sqrt(total_tokens))
    return (keys, input_grad, weight_grad)


def flip(index, distance):
    result = index
    bit = 1
    while bit <= distance:
        if distance & bit:
            result = result + bit - 2 * bit * lax.rem(lax.div(index, bit), 2)
        bit *= 2
    return result


def turn(values, cosine, signed_sine):
    parts = []
    for head in range(values.shape[1] // HEAD):
        piece = values[:, head * HEAD : (head + 1) * HEAD]
        parts.append(piece * cosine + pltpu.roll(piece, HEAD // 2, 1) * signed_sine)
    return jnp.concatenate(parts, axis=1)


CORES = 2
DEPTH = 4
GROUPS = (('S1', 'S1'), ('Q2z', 'Q2z'))
OVER = ((0, 0, (0, 0)), (0, 1, (0, 0)), (1, 0, (0, 0)), (1, 1, (0, 0)))
ROUTES = {
    "S1": {
        (0, 0): ("x", {"z": (1, 0), "y": (0, 1)}),
        (1, 0): ("z", {"y": (1, 1)}),
        (0, 1): ("y", {}),
        (1, 1): ("y", {}),
    },
    "S2": {
        (0, 0): ("x", {"y": (0, 1), "z": (1, 0)}),
        (0, 1): ("y", {"z": (1, 1)}),
        (1, 0): ("z", {}),
        (1, 1): ("z", {}),
    },
    "Q2z": {
        (0, 0): ("x", {"z": (1, 0)}),
        (0, 1): ("x", {"z": (1, 1)}),
        (1, 0): ("z", {}),
        (1, 1): ("z", {}),
    },
    "Q2y": {
        (0, 0): ("x", {"y": (0, 1)}),
        (1, 0): ("x", {"y": (1, 1)}),
        (0, 1): ("y", {}),
        (1, 1): ("y", {}),
    },
}
KEYS = ((0, 0), (0, 1), (1, 0), (1, 1))
SPLIT = 2
PARTS = len(GROUPS[0])
ORDER = (
    "exp", "bar", "xw1:00.0", "trg", "ypre", "xw1:01.1", "deq", "cpre",
    "cw", "xw0:00.0", "yc3f", "xw0:00.1", "p3", "w1:00.0", "yc2f", "p1",
    "ccols", "yc3n", "yc1f", "xw1:00.1", "p2", "w1:01.1", "rpre", "g3f",
    "yc2n", "p0", "yc0f", "yc1n", "g2f", "g3n", "w0:00.0", "s00e",
    "w0:00.1", "u0:00", "s01e", "o3", "w1:00.1", "g2n", "xw1:01.0", "g1f",
    "s10e", "w0:10.0", "s00i", "s11e", "w0:10.1", "v1:00", "g0f", "w1:10.0",
    "s01i", "w1:01.0", "yc0n", "v0:00", "g1n", "w1:10.1", "w1:11.1", "o2",
    "s20e", "s10i", "s20i", "o1", "w0:01.0", "w0:01.1", "v1:01", "s21e",
    "s11i", "s21i", "u1:01", "u1:00", "v0:10", "w1:11.0", "u0:10", "u1:11",
    "v1:10", "w0:11.0", "u0:01", "u1:10", "o0", "w0:11.1", "u0:11", "v1:11",
    "v0:01", "v0:11", "key", "g0n", "fin",
)


def fused_kernel(
    tokens_hbm,
    codes_hbm,
    exponents_hbm,
    cotangent_hbm,
    inverse_hbm,
    keys_ref,
    input_grad_ref,
    weight_grad_ref,
    tokens,
    codes,
    exponents_ref,
    cotangent_ref,
    inverse_ref,
    scale_ref,
    rotation,
    columns,
    pre,
    weights,
    out_x,
    in_x,
    out_z,
    in_z,
    kept,
    projected,
    load_sem,
    own_sem,
    column_send,
    column_recv,
    pre_send,
    pre_recv,
    own_send,
    own_recv,
    weight_send,
    weight_recv,
    sum_send,
    sum_recv,
    line_send,
    line_recv,
):
    node = lax.axis_index("node")
    local = lax.axis_index("local")
    nodes = lax.axis_size("node")
    locals_ = lax.axis_size("local")
    count = tokens.shape[0]
    row_count = columns.shape[2]
    shard_rows = weights.shape[1]
    features = pre.shape[1]
    unit_rows = shard_rows // (len(KEYS) * len(GROUPS))
    part_rows = unit_rows // PARTS
    width = features // SPLIT
    total = count * nodes * locals_

    depth_at = lax.div(node, 2)
    inner = lax.div(depth_at * (DEPTH - 1 - depth_at), 2)
    peers = {
        "c": (node, flip(local, 1)),
        "x": (node, flip(local, 2)),
        "y": (flip(node, 1), local),
        "d": (flip(node, 1), flip(local, 1)),
        "z": (flip(node, 2), local),
    }
    neighbours = len(peers)
    barrier = pltpu.get_barrier_semaphore()
    for peer in peers.values():
        pl.semaphore_signal(barrier, inc=1, device_id=peer, device_id_type=MESH)
    peers["m"] = (flip(node, 6), local)

    @pl.when(inner == 1)
    def _():
        pl.semaphore_signal(barrier, inc=1, device_id=peers["m"], device_id_type=MESH)

    def owned(r, far, e=0, d=0):
        first = (flip(node, 2 * r + e) * locals_ + flip(local, 2 * far + d)) * row_count
        return pl.ds(pl.multiple_of(first, row_count), row_count)

    def slot_rows(slot):
        return pl.ds(slot * count, count)

    def lanes_of(k):
        return pl.ds(k * width, width)

    zbit = lax.rem(depth_at, 2)
    ybit = lax.rem(node, 2)

    def unit_first(group, key):
        zz = 1 - zbit if key[0] else zbit
        yy = 1 - ybit if key[1] else ybit
        return pl.multiple_of((len(KEYS) * group + 2 * zz + yy) * unit_rows, unit_rows)

    def sem_index(group, key):
        return len(KEYS) * group + 2 * key[0] + key[1]

    def load(source, target, at):
        copy = pltpu.make_async_copy(source, target, load_sem.at[at])
        copy.start()
        return copy

    load_exponents = load(exponents_hbm, exponents_ref, 0)
    load_codes = {}
    keys = [(g, key) for g in range(len(GROUPS)) for key in KEYS]
    first_keys = [
        (g, key) for g, key in keys if any(ROUTES[kind][key][0] == "x" for kind in GROUPS[g])
    ]
    rest_keys = [pair for pair in keys if pair not in first_keys]

    def start_codes(pairs):
        for g, key in pairs:
            rows = pl.ds(unit_first(g, key), unit_rows)
            load_codes[g, key] = load(
                codes_hbm.at[rows, :], codes.at[rows, :], 4 + sem_index(g, key)
            )

    start_codes(first_keys)
    load_inverse = load(inverse_hbm, inverse_ref, 1)
    load_cotangent = load(cotangent_hbm, cotangent_ref, 2)
    start_codes(rest_keys)
    load_tokens = load(tokens_hbm, tokens, 3)
    own = {}
    for r in range(DEPTH - 1, -1, -1):
        for far in range(1, -1, -1):
            k = 2 * r + far
            own[k] = pltpu.make_async_copy(
                tokens_hbm.at[:, owned(r, far)], columns.at[k, slot_rows(0), :], own_sem.at[k]
            )
            own[k].start()

    def rotations():
        start = lax.rem((node * locals_ + local) * count, SEQ)
        positions = lax.rem(start + lax.broadcasted_iota(jnp.int32, (count, HEAD), 0), SEQ)
        load_inverse.wait()
        angles = positions.astype(jnp.float32) * inverse_ref[...]
        cosine = jnp.cos(angles)
        sine = jnp.sin(angles)
        lane = lax.broadcasted_iota(jnp.int32, (count, HEAD), 1)
        signed_sine = jnp.where(lane < HEAD // 2, -sine, sine)
        rotation[0] = cosine
        rotation[1] = signed_sine
        load_cotangent.wait()
        pre[slot_rows(0), :] = turn(
            cotangent_ref[...].astype(jnp.float32), cosine, -signed_sine
        ).astype(jnp.bfloat16)

    def scales():
        load_exponents.wait()
        scale = jnp.left_shift(1, exponents_ref[...] + 15).astype(jnp.float32) * (2.0**-15)
        scale_ref[...] = jnp.transpose(jnp.concatenate([scale] * (8 // scale.shape[0]), axis=0))

    def expand(group, key):
        load_codes[group, key].wait()
        rows = pl.ds(unit_first(group, key), unit_rows)
        for block in range(features // QBLOCK):
            lanes = pl.ds(block * QBLOCK, QBLOCK)
            weights[0, rows, lanes] = (
                codes[rows, lanes].astype(jnp.float32) * scale_ref[rows, block : block + 1]
            ).astype(jnp.bfloat16)

    sends = []
    waits = {}

    def describe(src, dst, send_sem, recv_sem, peer):
        return pltpu.make_async_remote_copy(
            src_ref=src,
            dst_ref=dst,
            send_sem=send_sem,
            recv_sem=recv_sem,
            device_id=peers[peer],
            device_id_type=MESH,
        )

    inner_sends = []

    def send(src, dst, send_sem, recv_sem, peer, only=None):
        copy = describe(src, dst, send_sem, recv_sem, peer)
        if only is None:
            copy.start()
            sends.append(copy)
        else:
            only.append(copy)

            @pl.when(inner == 1)
            def _():
                copy.start()

        return copy

    def send_columns(name, slot, peer, r, far, e, d):
        k = 2 * r + far
        waits[name, k] = send(
            tokens_hbm.at[:, owned(r, far, e, d)],
            columns.at[k, slot_rows(slot), :],
            column_send.at[k, slot],
            column_recv.at[k, slot],
            peer,
        )

    def send_pre(source, slot, peer):
        waits["pre", slot] = send(
            pre.at[slot_rows(source), :],
            pre.at[slot_rows(slot), :],
            pre_send.at[slot],
            pre_recv.at[slot],
            peer,
        )

    blocks = 4
    block_rows = shard_rows // blocks

    def use(slot, first, length):
        rows = pl.ds(pl.multiple_of(first, length), length)
        lane_first = flip(local, slot) * shard_rows + first
        lanes = pl.ds(pl.multiple_of(lane_first, length), length)
        block = weights[slot, rows, :]
        input_grad_ref[:, lanes] = lax.dot_general(
            pre[slot_rows(0), :],
            block,
            (((1,), (1,)), ((), ())),
            preferred_element_type=jnp.float32,
        ).astype(jnp.bfloat16)
        projected[...] += jnp.dot(
            tokens[:, lanes], block, preferred_element_type=jnp.float32
        )

    def send_unit(source, slot, group, source_key, key, part, peer):
        first = unit_first(group, source_key) + part * part_rows
        rows = pl.ds(pl.multiple_of(first, part_rows), part_rows)
        lane_of = {"x": 0, "y": 1, "z": 2, "c": 3, "m": 4}[peer]
        only = inner_sends if peer in "zm" and (group, part, source_key) in OVER else None
        waits["w", slot, group, key, part] = send(
            weights.at[source, rows, :],
            weights.at[slot, rows, :],
            weight_send.at[lane_of, sem_index(group, source_key), part],
            weight_recv.at[slot - 2, sem_index(group, key), part],
            peer,
            only,
        )

    def piece(r, far):
        k = 2 * r + far
        own[k].wait()
        for name in "cyd":
            waits[name, k].wait_recv()
        return lax.dot_general(
            columns[k], pre[...], (((0,), (0,)), ((), ())), preferred_element_type=jnp.float32
        )

    line = {}
    for i in range(DEPTH - 1):
        for k in range(SPLIT):
            for middle in range(2):
                slot = i + DEPTH - 1 if middle and i < 2 else i
                line[middle, i, k] = describe(
                    out_z.at[i * SPLIT + k],
                    in_z.at[slot * SPLIT + k],
                    line_send.at[i * SPLIT + k],
                    line_recv.at[slot * SPLIT + k],
                    "m" if middle and i < 2 else "z",
                )
    order_of = ((3, 2, 1), (2, 3, 1))

    def chain(i, k, places):
        for middle in places:

            @pl.when(inner == middle)
            def _():
                r = order_of[middle][i]
                waits["x", r, k].wait_recv()
                value = kept[r, :, lanes_of(k)] + in_x[r * SPLIT + k].astype(jnp.float32)
                if middle:
                    line[0 if i < 2 else 1, i if i < 2 else 0, k].wait_recv()
                    slot = i if i < 2 else DEPTH - 1
                    value = value + in_z[slot * SPLIT + k].astype(jnp.float32)
                out_z[i * SPLIT + k] = value.astype(jnp.bfloat16)
                line[middle, i, k].start()

    gain = 1.0 / math.sqrt(total)

    def finish(k):
        waits["x", 0, k].wait_recv()
        summed = kept[0, :, lanes_of(k)] + in_x[k].astype(jnp.float32)
        line[0, 2, k].wait_recv()
        summed = summed + in_z[2 * SPLIT + k].astype(jnp.float32)
        weight_grad_ref[:, lanes_of(k)] = summed * gain

        @pl.when(inner == 1)
        def _():
            line[1, 1, k].wait_recv()
            last = in_z[DEPTH * SPLIT + k].astype(jnp.float32)
            weight_grad_ref[:, lanes_of(k)] += last * gain

    pre_ready = []

    def run(step):
        head, _, rest = step.partition(":")
        if step == "ypre":
            send_pre(0, 2, "y")
        elif step == "cpre":
            send_pre(0, 1, "c")
        elif step == "exp":
            scales()
            for group, key in first_keys:
                expand(group, key)
        elif step == "trg":
            rotations()
        elif step == "deq":
            for group, key in rest_keys:
                expand(group, key)
            load_tokens.wait()
            projected[...] = jnp.zeros_like(projected)
        elif step == "rpre":
            waits["pre", 2].wait_recv()
            send_pre(2, 3, "c")
        elif step == "ccols":
            for r in (3, 2, 1, 0):
                for far in (1, 0):
                    send_columns("c", 1, "c", r, far, 0, 1)
        elif step == "cw":
            for b in range(blocks):
                rows = pl.ds(b * block_rows, block_rows)
                waits["own", b] = send(
                    weights.at[0, rows, :],
                    weights.at[1, rows, :],
                    own_send.at[b],
                    own_recv.at[b],
                    "c",
                )
        elif head[:2] == "yc":
            r, far = int(head[2]), int(head[3] == "f")
            send_columns("y", 2, "y", r, far, 1, 0)
            send_columns("d", 3, "d", r, far, 1, 1)
        elif head[:2] == "xw":
            group, key = int(head[2:]), (int(rest[0]), int(rest[1]))
            send_unit(0, 2, group, key, key, int(rest[3]), "x")
        elif head[0] == "o":
            use(0, int(head[1]) * block_rows, block_rows)
        elif head[0] == "p":
            waits["own", int(head[1])].wait_recv()
            use(1, int(head[1]) * block_rows, block_rows)
        elif head[0] == "w":
            group, key = int(head[1:]), (int(rest[0]), int(rest[1]))
            part = int(rest[3])
            waits["w", 2, group, key, part].wait_recv()
            for peer, there in ROUTES[GROUPS[group][part]][key][1].items():
                send_unit(2, 2, group, key, there, part, peer)
                if peer == "z" and (group, part, key) in OVER:
                    send_unit(2, 2, group, key, there, part, "m")
            send_unit(2, 3, group, key, key, part, "c")
        elif head[0] in "uv":
            group, key = int(head[1:]), (int(rest[0]), int(rest[1]))
            slot = 2 if head[0] == "u" else 3
            if slot == 3:
                for part in range(PARTS):
                    waits["w", 3, group, key, part].wait_recv()
            use(slot, unit_first(group, key), unit_rows)
        elif head[0] == "g":
            r, far = int(head[1]), int(head[2] == "f")
            if not pre_ready:
                waits["pre", 1].wait_recv()
                waits["pre", 3].wait_recv()
                pre_ready.append(True)
            value = piece(r, far)
            if far:
                for k in range(SPLIT):
                    at = r * SPLIT + k
                    out_x[at] = value[:, k * width : (k + 1) * width].astype(jnp.bfloat16)
                    waits["x", r, k] = send(
                        out_x.at[at], in_x.at[at], sum_send.at[at], sum_recv.at[at], "x"
                    )
            else:
                kept[r] = value
        elif head[0] == "s":
            chain(int(head[1]), int(head[2]), ("ei".index(head[3]),))
        elif step == "key":
            keys_ref[...] = turn(projected[...], rotation[0], rotation[1]).astype(jnp.bfloat16)
        elif step == "fin":
            for k in range(SPLIT):
                finish(k)
        elif step == "bar":
            pl.semaphore_wait(barrier, neighbours + inner)
        else:
            raise ValueError(step)

    steps = ORDER
    if "bar" not in steps:
        run("bar")
    for step in steps:
        run(step)
    for copy in sends:
        copy.wait_send()

    @pl.when(inner == 1)
    def _():
        for copy in inner_sends:
            copy.wait_send()

    for middle in range(2):

        @pl.when(inner == middle)
        def _():
            for i in range(DEPTH - 1):
                for k in range(SPLIT):
                    line[middle, i, k].wait_send()


def place(*refs):
    copies = [pltpu.make_async_copy(refs[i], refs[3 + i], refs[6].at[i]) for i in range(3)]
    for copy in copies:
        copy.start()
    for copy in copies:
        copy.wait()


def fused(tokens, key_codes, key_exponents, key_cotangent):
    nodes = lax.axis_size("node")
    locals_ = lax.axis_size("local")
    count, width = tokens.shape
    shard_rows, features = key_codes.shape
    row_count = width // (nodes * locals_)
    units = len(KEYS) * len(GROUPS)
    half = THETA ** (-(np.arange(HEAD // 2) * 2.0 / HEAD))
    inverse = jnp.asarray(np.concatenate([half, half])[None, :], jnp.float32)
    anywhere = pl.BlockSpec(memory_space=pl.ANY)
    vmem = pl.BlockSpec(memory_space=pltpu.VMEM)
    dma = pltpu.SemaphoreType.DMA
    held = pl.pallas_call(
        fused_kernel,
        out_shape=(
            pltpu.VMEM((count, features), jnp.bfloat16),
            pltpu.VMEM((count, width), jnp.bfloat16),
            pltpu.VMEM((row_count, features), jnp.float32),
        ),
        in_specs=[anywhere] * 5,
        out_specs=(vmem, vmem, vmem),
        scratch_shapes=[
            pltpu.VMEM((count, width), jnp.bfloat16),
            pltpu.VMEM((shard_rows, features), jnp.bfloat16),
            pltpu.VMEM(key_exponents.shape[::-1], jnp.int32),
            pltpu.VMEM((count, features), jnp.bfloat16),
            pltpu.VMEM((1, HEAD), jnp.float32),
            pltpu.VMEM((shard_rows, 8), jnp.float32),
            pltpu.VMEM((2, count, HEAD), jnp.float32),
            pltpu.VMEM((2 * DEPTH, locals_ * count, row_count), jnp.bfloat16),
            pltpu.VMEM((locals_ * count, features), jnp.bfloat16),
            pltpu.VMEM((locals_, shard_rows, features), jnp.bfloat16),
            pltpu.VMEM((DEPTH * SPLIT, row_count, features // SPLIT), jnp.bfloat16),
            pltpu.VMEM((DEPTH * SPLIT, row_count, features // SPLIT), jnp.bfloat16),
            pltpu.VMEM((3 * SPLIT, row_count, features // SPLIT), jnp.bfloat16),
            pltpu.VMEM((5 * SPLIT, row_count, features // SPLIT), jnp.bfloat16),
            pltpu.VMEM((DEPTH, row_count, features), jnp.float32),
            pltpu.VMEM((count, features), jnp.float32),
            dma((4 + units,)),
            dma((2 * DEPTH,)),
            dma((2 * DEPTH, 4)),
            dma((2 * DEPTH, 4)),
            dma((4,)),
            dma((4,)),
            dma((4,)),
            dma((4,)),
            dma((5, units, PARTS)),
            dma((2, units, PARTS)),
            dma((DEPTH * SPLIT,)),
            dma((DEPTH * SPLIT,)),
            dma((3 * SPLIT,)),
            dma((5 * SPLIT,)),
        ],
        compiler_params=pltpu.CompilerParams(collective_id=0, has_side_effects=True),
    )(tokens, key_codes, key_exponents.T, key_cotangent, inverse)
    return pl.pallas_call(
        place,
        out_shape=tuple(jax.ShapeDtypeStruct(a.shape, a.dtype) for a in held),
        in_specs=[vmem] * 3,
        out_specs=(anywhere,) * 3,
        scratch_shapes=[dma((3,))],
    )(*(pltpu.with_memory_space_constraint(a, pltpu.VMEM) for a in held))


def solution(mesh):
    def body(tokens, key_codes, key_exponents, key_cotangent):
        nodes, locals_ = mesh.shape["node"], mesh.shape["local"]
        row_count = tokens.shape[1] // (nodes * locals_)
        grid = nodes == 2 * DEPTH and locals_ == 2 * CORES
        run = fused if grid and row_count % HEAD == 0 else on_device
        return run(tokens, key_codes, key_exponents, key_cotangent)

    return jax.shard_map(
        body,
        mesh=mesh,
        in_specs=(
            P(("node", "local"), None),
            P("local", None),
            P("local", None),
            P(("node", "local"), None),
        ),
        out_specs=(
            P(("node", "local"), None),
            P(("node", "local"), None),
            P(("node", "local"), None),
        ),
        check_vma=False,
    )
```
